32 devices in a mesh: nodes: 16 (over z, y, x), orb: 2 (over core).
Axes of the slice: x: 2, y: 2, z: 4, core: 2. Of those that a mesh axis runs over, the one named last changes fastest.
Arguments:
- orbitals: float32 [10368, 2048], P('nodes', 'orb'), may hold values from -60 to 60
- cell_matrix: float32 [16, 729, 729], P('nodes'), may hold values from -0.25 to 1.75
- connectivity: int32 [16, 729], P('nodes'), may hold values from 0 to 728, as said below
- face_nodes: int32 [1296], P('nodes'), may hold values from 0 to 647, as said below
Outputs:
- rotated: float32 [10368, 2048], P('nodes', 'orb')
The draws below stay inside these ranges and needn't reach their ends.
Inputs may be any that keep to these rules, and one draw needn't show every extreme that they name: `connectivity`: within a section, entries below 648 are local node numbers and entry 648 + g is ghost slot g; the entries of one cell are distinct, and every local node and every ghost slot of a section appears in some cell of it. Ghost slots appear only in the last cell of a section. `face_nodes`: the 81 entries of a section are distinct local node numbers, listed in the order of the ghost slots of the section below.
All inputs are finite; a program needn't handle non-finite values.
Results may differ from the reference program's by a relative error of at most 0.000088.
Values sent between devices are 32-bit elements; how exact they have to be, the bound alone decides.
No kernel may reach another device: no remote copies, remote signals or barrier semaphores. Data moves between devices by JAX's collectives and lax.ppermute only.
A program may use at most 128 MiB of HBM per device.

```python
import math
import jax
import jax.numpy as jnp
from jax import lax

SIDE = 9
ORBS = 2048
DEGREE = 8
CELLS_DEV = 1
CELL_NODES = 729
FACE = 81
NODES_DEV = 648
NODES = 10368
CELLS = 16
N_NODES = 16


def section_perms(key):
    sections = CELLS // CELLS_DEV
    keys = jax.random.split(jax.random.fold_in(key, 11), sections)
    return jax.vmap(lambda sub: jax.random.permutation(sub, NODES_DEV))(keys).astype(jnp.int32)


def draw_connectivity(key, part):
    perms = section_perms(key)
    layers = (SIDE - 1) * CELLS_DEV
    cell = jnp.arange(CELLS, dtype=jnp.int32)
    section = cell // CELLS_DEV
    within = cell % CELLS_DEV
    node = jnp.arange(CELL_NODES, dtype=jnp.int32)
    first = node // FACE
    second = node // SIDE % SIDE
    third = node % SIDE
    plane = first * SIDE + second
    layer = within[:, None] * (SIDE - 1) + third[None, :]
    structured = layer * FACE + plane[None, :]
    local = perms[section[:, None], jnp.minimum(structured, NODES_DEV - 1)]
    return jnp.where(layer < layers, local, NODES_DEV + plane[None, :]).astype(jnp.int32)


def draw_face_nodes(key, part):
    perms = section_perms(key)
    return perms[:, :FACE].reshape(-1).astype(jnp.int32)


def draw_cell_matrix(key, part):
    first, second = jax.random.split(jax.random.fold_in(key, 5), 2)
    spread = 0.25 / math.sqrt(CELL_NODES)
    noise = jnp.clip(jax.random.normal(first, (CELLS, CELL_NODES, CELL_NODES), jnp.float32), -3.0, 3.0)
    symmetric = (noise + jnp.swapaxes(noise, 1, 2)) * (spread / math.sqrt(2.0))
    diagonal = jnp.exp(jax.random.uniform(second, (CELLS, CELL_NODES), jnp.float32, math.log(0.3), math.log(1.5)))
    return symmetric + diagonal[:, :, None] * jnp.eye(CELL_NODES, dtype=jnp.float32)[None]


def draw_orbitals(key, part):
    first, second, third = jax.random.split(jax.random.fold_in(key, 3), 3)
    base = jnp.clip(jax.random.normal(first, (NODES, ORBS), jnp.float32), -4.0, 4.0)
    position = jnp.arange(NODES, dtype=jnp.float32) / max(NODES - 1, 1)
    rising = jnp.sqrt(1.0 + 2.0 * position) * jnp.exp(jax.random.uniform(second, (NODES,), jnp.float32, -0.4, 0.4))
    columns = jnp.exp(jax.random.uniform(third, (ORBS,), jnp.float32, -0.4, 0.4))
    return base * rising[:, None] * columns[None, :]


def setup_inputs(seed: int = 0) -> dict:
    splits = jax.random.split(jax.random.key(seed), 5)
    orbitals = draw_orbitals(jax.random.fold_in(splits[4], 71), 0)
    cell_matrix = draw_cell_matrix(jax.random.fold_in(splits[4], 71), 0)
    connectivity = draw_connectivity(jax.random.fold_in(splits[4], 71), 0)
    face_nodes = draw_face_nodes(jax.random.fold_in(splits[4], 71), 0)
    return {"orbitals": orbitals, "cell_matrix": cell_matrix, "connectivity": connectivity, "face_nodes": face_nodes}


lowest = -1.0
cutoff = 1.5
ceiling = 4.5
eps_norm = 1e-06

def chebyshev(start, apply_fn):
    half_width = (ceiling - cutoff) / 2.0
    centre = (ceiling + cutoff) / 2.0
    sigma_one = half_width / (lowest - centre)
    prev = start
    cur = (apply_fn(prev) - centre * prev) * (sigma_one / half_width)
    sigma_now = sigma_one
    for degree_step in range(DEGREE - 1):
        sigma_next = 1.0 / (2.0 / sigma_one - sigma_now)
        fresh = (apply_fn(cur) - centre * cur) * (2.0 * sigma_next / half_width) - sigma_now * sigma_next * prev
        prev = cur
        cur = fresh
        sigma_now = sigma_next
    return cur

def reference(orbitals, cell_matrix, connectivity, face_nodes):
    section = (jnp.arange(CELLS, dtype=jnp.int32) // CELLS_DEV)[:, None]
    face_all = face_nodes.reshape(N_NODES, FACE)
    above = jnp.minimum(section + 1, N_NODES - 1).astype(jnp.int32)
    slot = jnp.clip(connectivity - NODES_DEV, 0, FACE - 1).astype(jnp.int32)
    ghost_target = (section + 1) * NODES_DEV + face_all[above, slot]
    has_above = section + 1 < N_NODES
    global_index = jnp.where(connectivity < NODES_DEV, section * NODES_DEV + connectivity, jnp.where(has_above, ghost_target, NODES)).astype(jnp.int32)
    flat_index = global_index.reshape(-1)

    def apply_ham(field):
        extended = jnp.concatenate([field, jnp.zeros((1, ORBS), jnp.float32)], axis=0)
        local = extended[global_index]
        product = jnp.einsum('cij,cjo->cio', cell_matrix, local, precision=lax.Precision.HIGHEST)
        summed = jnp.zeros((NODES + 1, ORBS), jnp.float32).at[flat_index].add(product.reshape(-1, ORBS))
        return summed[:NODES]
    filtered = chebyshev(orbitals, apply_ham)
    intersection = jnp.dot(filtered.T, filtered, precision=lax.Precision.HIGHEST)
    scale = lax.rsqrt(jnp.diagonal(intersection) / NODES + eps_norm)
    unit = filtered * scale[None, :]
    coupling = intersection * scale[:, None] * scale[None, :] / NODES
    return 1.5 * unit - 0.5 * jnp.dot(unit, coupling, precision=lax.Precision.HIGHEST)
```

```python
import jax
import jax.numpy as jnp
from jax import lax
from jax.experimental import pallas as pl
from jax.experimental.pallas import tpu as pltpu
from jax.sharding import PartitionSpec as P

DEGREE = 8
CHUNKS = 2

lowest = -1.0
cutoff = 1.5
ceiling = 4.5
eps_norm = 1e-06

F32 = jnp.float32
BF16 = jnp.bfloat16
VMEM = pl.BlockSpec(memory_space=pltpu.VMEM)
LIMIT = 18 * 1024 * 1024


def up_to(value, unit):
    return -(-value // unit) * unit


def split(value):
    high = value.astype(BF16)
    return high, (value - high.astype(F32)).astype(BF16)


def mm(left, right):
    return jnp.dot(left, right, preferred_element_type=F32)


def mm_nt(left, right):
    return lax.dot_general(left, right, (((1,), (1,)), ((), ())), preferred_element_type=F32)


def shifted(shard, axis, by):
    count = lax.axis_size(axis)
    pairs = [(i, i + by) for i in range(count) if 0 <= i + by < count]
    return lax.ppermute(shard, axis, pairs)


def coefficients():
    half_width = (ceiling - cutoff) / 2.0
    centre = (ceiling + cutoff) / 2.0
    sigma_one = half_width / (lowest - centre)
    pairs = [(sigma_one / half_width, 0.0)]
    sigma_now = sigma_one
    for _ in range(DEGREE - 1):
        sigma_next = 1.0 / (2.0 / sigma_one - sigma_now)
        pairs.append((2.0 * sigma_next / half_width, sigma_now * sigma_next))
        sigma_now = sigma_next
    return centre, pairs


class Layout:
    def __init__(self, owned, face):
        self.owned = owned
        self.face = face
        self.rest = up_to(owned - face, 8)
        self.fpad = up_to(face, 8)
        self.rows = up_to(self.rest + self.fpad, 16)
        self.ext = up_to(self.rows + self.fpad, 16)

    def position(self, ids, faces):
        same = ids[:, None] == faces[None, :]
        slot = jnp.sum(jnp.where(same, jnp.arange(self.face, dtype=jnp.int32)[None, :] + 1, 0), axis=1)
        below = jnp.sum((faces[None, :] < ids[:, None]).astype(jnp.int32), axis=1)
        own = jnp.where(slot > 0, self.rest + slot - 1, ids - below)
        return jnp.where(ids < self.owned, own, self.rows + ids - self.owned)


def arrange_kernel(lay, a_ref, q_ref, b_ref):
    cells, nodes, _ = a_ref.shape
    total = jnp.zeros((lay.ext, lay.ext), F32)
    for cell in range(cells):
        q = q_ref[cell]
        hot = (lax.broadcasted_iota(jnp.int32, (lay.ext, nodes), 0) == q).astype(F32).astype(BF16)
        for part in split(a_ref[cell]):
            total = total + mm_nt(mm(hot, part).astype(BF16), hot)
    b_ref[...] = total


def arrange(lay, matrices, q):
    return pl.pallas_call(
        lambda *refs: arrange_kernel(lay, *refs),
        out_shape=jax.ShapeDtypeStruct((lay.ext, lay.ext), F32),
        in_specs=[VMEM, VMEM],
        out_specs=VMEM,
        compiler_params=pltpu.CompilerParams(vmem_limit_bytes=LIMIT),
        name="arrange",
    )(matrices, q)


def outgoing(lay, bh, bl, value, face_ref, lift_ref):
    high, low = split(value)
    gh = bh[lay.rows : lay.rows + lay.fpad, : lay.rows]
    gl = bl[lay.rows : lay.rows + lay.fpad, : lay.rows]
    lift_ref[...] = mm(gh, high) + mm(gh, low) + mm(gl, high)
    face_ref[...] = value[lay.rest : lay.rest + lay.fpad]


def first_kernel(lay, bh_ref, bl_ref, cur_ref, face_ref, lift_ref):
    outgoing(lay, bh_ref, bl_ref, cur_ref[...], face_ref, lift_ref)


def step_kernel(lay, centre, alpha, beta, last, bh_ref, bl_ref, cur_ref, prev_ref, ghost_ref, add_ref, *outs):
    new_ref = outs[0]
    high_ref, low_ref = outs[-2:]
    rows, ext, fpad = lay.rows, lay.ext, lay.fpad
    cur = cur_ref[...]
    high_ref[:rows], low_ref[:rows] = split(cur)
    ghost = ghost_ref[...]
    if ext - rows > fpad:
        ghost = jnp.concatenate([ghost, jnp.zeros((ext - rows - fpad, ghost.shape[1]), F32)], axis=0)
    high_ref[rows:], low_ref[rows:] = split(ghost)
    bh = bh_ref[:rows]
    value = mm(bh, high_ref[...]) + mm(bh, low_ref[...]) + mm(bl_ref[:rows], high_ref[...])
    new = (value - centre * cur) * alpha
    if beta:
        new = new - beta * prev_ref[...]
    new_ref[...] = new
    new_ref[lay.rest : lay.rest + fpad] += alpha * add_ref[...]
    if not last:
        outgoing(lay, bh_ref, bl_ref, new_ref[...], outs[1], outs[2])


def cost(lay, width):
    return pl.CostEstimate(
        flops=6 * lay.ext * lay.ext * width, bytes_accessed=3 * 4 * lay.rows * width, transcendentals=0
    )


def first(lay, bh, bl, cur):
    width = cur.shape[1]
    part = jax.ShapeDtypeStruct((lay.fpad, width), F32)
    return pl.pallas_call(
        lambda *refs: first_kernel(lay, *refs),
        out_shape=[part, part],
        in_specs=[VMEM] * 3,
        out_specs=[VMEM] * 2,
        compiler_params=pltpu.CompilerParams(vmem_limit_bytes=LIMIT),
        cost_estimate=cost(lay, width // 8),
        name="first",
    )(bh, bl, cur)


def advance(lay, centre, alpha, beta, last, bh, bl, cur, prev, ghost, add):
    width = cur.shape[1]
    part = jax.ShapeDtypeStruct((lay.fpad, width), F32)
    outs = [jax.ShapeDtypeStruct((lay.rows, width), F32)]
    if not last:
        outs += [part, part]
    return pl.pallas_call(
        lambda *refs: step_kernel(lay, centre, alpha, beta, last, *refs),
        out_shape=outs,
        in_specs=[VMEM] * 6,
        out_specs=[VMEM] * len(outs),
        scratch_shapes=[pltpu.VMEM((lay.ext, width), BF16)] * 2,
        compiler_params=pltpu.CompilerParams(vmem_limit_bytes=LIMIT),
        cost_estimate=cost(lay, width),
        name="step",
    )(bh, bl, cur, prev, ghost, add)


def filter_chunks(lay, bh, bl, chunks):
    centre, pairs = coefficients()
    states = []
    for cur in chunks:
        face, lift = first(lay, bh, bl, cur)
        states.append((cur, cur, face, lift))
    for degree, (alpha, beta) in enumerate(pairs):
        last = degree == len(pairs) - 1
        fresh = []
        for cur, prev, face, lift in states:
            ghost = shifted(face, "nodes", -1)
            add = shifted(lift, "nodes", 1)
            outs = advance(lay, centre, alpha, beta, last, bh, bl, cur, prev, ghost, add)
            fresh.append((outs[0], cur) + tuple(outs[1:]))
        states = fresh
    return [state[0] for state in states]


def inner(left, right):
    return jnp.einsum("no,nq->oq", left, right, precision=lax.Precision.HIGH)


def orthonormalize_ring(filtered, place, owned):
    width = filtered.shape[1]
    total_rows = owned * lax.axis_size("nodes")
    members = lax.axis_size("orb")
    position = lax.axis_index("orb")
    blocks = [filtered]
    for stride in range(1, members // 2 + 1):
        pairs = [(source, (source + stride) % members) for source in range(members)]
        blocks.append(lax.ppermute(filtered, "orb", pairs))
    tiles = lax.psum(jnp.stack([inner(filtered, block) for block in blocks]), "nodes")
    eye = jnp.eye(width, dtype=jnp.bool_)
    diag_own = jnp.sum(jnp.where(eye, tiles[0], 0.0), axis=0)
    diag_all = lax.all_gather(diag_own, "orb", axis=0, tiled=True)
    scale_all = lax.rsqrt(diag_all / total_rows + eps_norm)
    scale_own = lax.rsqrt(diag_own / total_rows + eps_norm)
    unit_own = filtered * scale_own[None, :]
    mixed = jnp.zeros(filtered.shape, F32)
    for stride in range(members // 2 + 1):
        source = (position - stride) % members
        scale_source = lax.dynamic_slice_in_dim(scale_all, source * width, width, 0)
        coupling = tiles[stride] * scale_own[:, None] * scale_source[None, :] / total_rows
        mixed = mixed + jnp.dot(
            blocks[stride] * scale_source[None, :], coupling.T, precision=lax.Precision.HIGH
        )
        if stride > 0 and 2 * stride != members:
            returned = jnp.dot(unit_own, coupling, precision=lax.Precision.HIGH)
            pairs = [(source, (source - stride) % members) for source in range(members)]
            mixed = mixed + lax.ppermute(returned, "orb", pairs)
    rotated = 1.5 * unit_own - 0.5 * mixed
    return rotated[place]


def mm_tn(left, right):
    return lax.dot_general(left, right, (((0,), (0,)), ((), ())), preferred_element_type=F32)


def triple(product, left, right):
    return product(left[0], right[0]) + product(left[0], right[1]) + product(left[1], right[0])


QUARTERS = 4
OWN_BLOCKS = [(i, j) for i in range(QUARTERS) for j in range(i, QUARTERS)]
COLOUR_BLOCKS = 6


def own_gram_kernel(bs, a_ref, b_ref, c0_ref, c1_ref):
    low, high = split(a_ref[...]), split(b_ref[...])
    parts = []
    for source in (low, high):
        for quarter in range(2):
            parts.append(tuple(piece[:, quarter * bs : (quarter + 1) * bs] for piece in source))
    for index, (i, j) in enumerate(OWN_BLOCKS):
        ref, slot = (c0_ref, index) if index < COLOUR_BLOCKS else (c1_ref, index - COLOUR_BLOCKS)
        ref[slot * bs : (slot + 1) * bs] = triple(mm_tn, parts[i], parts[j])


def cross_gram_kernel(bs, o_ref, a_ref, b_ref, oa_ref, ob_ref, c1_ref, c2_ref, norm_ref):
    same = o_ref[0] == 0
    own = (a_ref[...], b_ref[...])
    other = (oa_ref[...], ob_ref[...])
    slot = 0
    for half in range(2):
        left = split(own[half])
        right = split(jnp.where(same, other[half], other[1 - half]))
        for r in range(2):
            rows = triple(mm_tn, tuple(piece[:, r * bs : (r + 1) * bs] for piece in left), right)
            for k in range(2):
                ref, at = (c1_ref, slot) if slot < 2 else (c2_ref, slot - 2)
                ref[at * bs : (at + 1) * bs] = rows[:, k * bs : (k + 1) * bs]
                slot += 1
    for index, value in enumerate(own + other):
        total = jnp.sum(value * value, axis=0, keepdims=True)
        for k in range(2):
            norm_ref[2 * index + k : 2 * index + k + 1] = total[:, k * bs : (k + 1) * bs]


def own_gram(a, b, bs):
    return pl.pallas_call(
        lambda *refs: own_gram_kernel(bs, *refs),
        out_shape=[
            jax.ShapeDtypeStruct((COLOUR_BLOCKS * bs, bs), F32),
            jax.ShapeDtypeStruct(((len(OWN_BLOCKS) - COLOUR_BLOCKS) * bs, bs), F32),
        ],
        in_specs=[VMEM] * 2,
        out_specs=[VMEM] * 2,
        compiler_params=pltpu.CompilerParams(vmem_limit_bytes=LIMIT),
        cost_estimate=pl.CostEstimate(flops=6 * 10 * a.shape[0] * bs * bs, bytes_accessed=4 * a.size, transcendentals=0),
        name="own_gram",
    )(a, b)


def cross_gram(core, a, b, oa, ob, bs):
    return pl.pallas_call(
        lambda *refs: cross_gram_kernel(bs, *refs),
        out_shape=[
            jax.ShapeDtypeStruct((2 * bs, bs), F32),
            jax.ShapeDtypeStruct((COLOUR_BLOCKS * bs, bs), F32),
            jax.ShapeDtypeStruct((8, bs), F32),
        ],
        in_specs=[pl.BlockSpec(memory_space=pltpu.SMEM)] + [VMEM] * 4,
        out_specs=[VMEM] * 3,
        compiler_params=pltpu.CompilerParams(vmem_limit_bytes=LIMIT),
        cost_estimate=pl.CostEstimate(flops=6 * 8 * a.shape[0] * bs * bs, bytes_accessed=8 * a.size, transcendentals=0),
        name="cross_gram",
    )(core, a, b, oa, ob)


def weigh_kernel(bs, total_rows, norm_ref, own_ref, other_ref, wh_ref, wl_ref, base_ref, scale_ref):
    for index, ref in enumerate((own_ref, other_ref)):
        for quarter in range(QUARTERS):
            norm = norm_ref[index * QUARTERS + quarter : index * QUARTERS + quarter + 1]
            scale = lax.rsqrt(norm / total_rows + eps_norm)
            columns = slice(quarter * bs, (quarter + 1) * bs)
            value = ref[:, columns]
            at = slice((index * QUARTERS + quarter) * bs, (index * QUARTERS + quarter + 1) * bs)
            wh_ref[:, at], wl_ref[:, at] = split(value * (scale * scale * (0.5 / total_rows)))
            if index == 0:
                base_ref[:, columns] = value * 1.5
                scale_ref[:, columns] = scale


def weigh(norms, own, other, bs, total_rows):
    rows, width = own.shape
    return pl.pallas_call(
        lambda *refs: weigh_kernel(bs, total_rows, *refs),
        out_shape=[
            jax.ShapeDtypeStruct((rows, 2 * width), BF16),
            jax.ShapeDtypeStruct((rows, 2 * width), BF16),
            jax.ShapeDtypeStruct((rows, width), F32),
            jax.ShapeDtypeStruct((1, width), F32),
        ],
        in_specs=[VMEM] * 3,
        out_specs=[VMEM] * 4,
        compiler_params=pltpu.CompilerParams(vmem_limit_bytes=LIMIT),
        cost_estimate=pl.CostEstimate(flops=8 * rows * width, bytes_accessed=24 * rows * width, transcendentals=0),
        name="weigh",
    )(norms, own, other)


def rotate_kernel(bs, o_ref, wh_ref, wl_ref, base_ref, scale_ref, c0_ref, c1_ref, c2_ref, p1_ref, p2_ref, out_ref):
    same = o_ref[0] == 0

    def block(ref, slot):
        return ref[slot * bs : (slot + 1) * bs]

    def own_block(i, j):
        index = OWN_BLOCKS.index((i, j))
        return block(c0_ref, index) if index < COLOUR_BLOCKS else block(c1_ref, index - COLOUR_BLOCKS)

    def cross(first_ref, first_at, second_ref, half, r, k):
        slot = half * 4 + r * 2 + k
        return block(first_ref, first_at + slot) if slot < 2 else block(second_ref, slot - 2)

    def weight(quarter):
        at = slice(quarter * bs, (quarter + 1) * bs)
        return wh_ref[:, at], wl_ref[:, at]

    def chosen(first, second):
        return tuple(jnp.where(same, x, y) for x, y in zip(first, second))

    for j in range(QUARTERS):
        half, inside = j // 2, j % 2
        total = base_ref[:, j * bs : (j + 1) * bs]
        for i in range(QUARTERS):
            if i <= j:
                total = total - triple(mm, weight(i), split(own_block(i, j)))
            else:
                total = total - triple(mm_nt, weight(i), split(own_block(j, i)))
        for k in range(2):
            near, far = weight(QUARTERS + 2 * half + k), weight(QUARTERS + 2 * (1 - half) + k)
            mine = split(cross(c1_ref, 4, c2_ref, half, inside, k))
            total = total - triple(mm_nt, chosen(near, far), mine)
            theirs = jnp.where(
                same, cross(p1_ref, 0, p2_ref, 1 - half, k, inside), cross(p1_ref, 0, p2_ref, half, k, inside)
            )
            total = total - triple(mm, chosen(far, near), split(theirs))
        out_ref[:, j * bs : (j + 1) * bs] = total * scale_ref[:, j * bs : (j + 1) * bs]


def rotate(core, weights, colours, partner, bs):
    rows, width = weights[2].shape
    return pl.pallas_call(
        lambda *refs: rotate_kernel(bs, *refs),
        out_shape=jax.ShapeDtypeStruct((rows, width), F32),
        in_specs=[pl.BlockSpec(memory_space=pltpu.SMEM)] + [VMEM] * 9,
        out_specs=VMEM,
        compiler_params=pltpu.CompilerParams(vmem_limit_bytes=LIMIT),
        cost_estimate=pl.CostEstimate(flops=12 * rows * width * width, bytes_accessed=16 * rows * width, transcendentals=0),
        name="rotate",
    )(core, *weights, *colours, *partner)


def exchange(value, axis, bit):
    count = lax.axis_size(axis)
    return lax.ppermute(value, axis, [(i, i ^ (1 << bit)) for i in range(count)])


def side(node, bit):
    return (node >> bit) & 1


def sum_over_nodes(colours, norms):
    count = lax.axis_size("nodes")
    node = lax.axis_index("nodes")
    bits = list(range(count.bit_length() - 1))
    ring = bits[:-1] if len(bits) > 1 else bits
    orders = []
    for index in range(len(colours)):
        turn = index % len(ring)
        orders.append(ring[turn:] + ring[:turn] + bits[len(ring) :])
    for phase in range(len(bits)):
        for index, order in enumerate(orders):
            value, bit = colours[index], order[phase]
            half = value.shape[0] // 2
            mine = side(node, bit) * half
            away = lax.dynamic_slice_in_dim(value, half - mine, half, 0)
            keep = lax.dynamic_slice_in_dim(value, mine, half, 0)
            if index == len(colours) - 1:
                got = exchange(jnp.concatenate([away, norms], axis=0), "nodes", bit)
                norms = norms + got[half:]
                colours[index] = keep + got[:half]
            else:
                colours[index] = keep + exchange(away, "nodes", bit)
    for phase in reversed(range(len(bits))):
        for index, order in enumerate(orders):
            value, bit = colours[index], order[phase]
            got = exchange(value, "nodes", bit)
            lower = side(node, bit) == 0
            colours[index] = jnp.concatenate([jnp.where(lower, value, got), jnp.where(lower, got, value)], axis=0)
    return colours, norms


def orthonormalize_pair(a, b, place, owned, bs):
    core = lax.axis_index("orb")
    index = core.reshape(1).astype(jnp.int32)
    oa, ob = exchange(a, "orb", 0), exchange(b, "orb", 0)
    c0, c1_own = own_gram(a, b, bs)
    c1_cross, c2, norms = cross_gram(index, a, b, oa, ob, bs)
    c1 = jnp.concatenate([c1_own, c1_cross], axis=0)
    colours, norms = sum_over_nodes([c0, c1, c2], norms)
    p1 = exchange(colours[1][4 * bs :], "orb", 0)
    p2 = exchange(colours[2], "orb", 0)
    own = jnp.concatenate([a, b], axis=1)[place]
    other = jnp.concatenate([oa, ob], axis=1)[place]
    weights = weigh(norms, own, other, bs, owned * lax.axis_size("nodes"))
    return rotate(index, weights, colours, [p1, p2], bs)


def body(orbitals, cell_matrix, connectivity, face_nodes):
    owned, width = orbitals.shape
    lay = Layout(owned, face_nodes.shape[0])
    cells, nodes = connectivity.shape
    place = lay.position(jnp.arange(owned, dtype=jnp.int32), face_nodes)
    q = lay.position(connectivity.reshape(-1), face_nodes).reshape(cells, 1, nodes)
    hit = place[None, :] == jnp.arange(lay.rows, dtype=jnp.int32)[:, None]
    order = jnp.sum(jnp.where(hit, jnp.arange(owned, dtype=jnp.int32)[None, :], 0), axis=1)
    valid = jnp.any(hit, axis=1)
    start = jnp.where(valid[:, None], orbitals[order], 0.0)

    matrix = arrange(lay, cell_matrix, q)
    corner = matrix[lay.rows : lay.rows + lay.fpad, lay.rows : lay.rows + lay.fpad]
    corner = shifted(corner, "nodes", 1)
    pad = (lay.rest, lay.ext - lay.rest - lay.fpad)
    matrix = matrix + jnp.pad(corner, (pad, pad))
    rounded = lax.reduce_precision(matrix, 8, 7)
    bh, bl = rounded.astype(BF16), (matrix - rounded).astype(BF16)

    step = width // CHUNKS
    parts = filter_chunks(lay, bh, bl, [start[:, i * step : (i + 1) * step] for i in range(CHUNKS)])
    count = lax.axis_size("nodes")
    bs = width // QUARTERS
    if lax.axis_size("orb") == 2 and CHUNKS == 2 and count & (count - 1) == 0 and bs % 128 == 0 and 6 * bs % (8 * count) == 0:
        return orthonormalize_pair(parts[0], parts[1], place, owned, bs)
    return orthonormalize_ring(jnp.concatenate(parts, axis=1), place, owned)


def solution(mesh):
    return jax.shard_map(
        body,
        mesh=mesh,
        in_specs=(P("nodes", "orb"), P("nodes", None, None), P("nodes", None), P("nodes")),
        out_specs=P("nodes", "orb"),
        check_vma=False,
    )
```

```python
import jax
import jax.numpy as jnp
from jax import lax
from jax.experimental import pallas as pl
from jax.experimental.pallas import tpu as pltpu
from jax.sharding import PartitionSpec as P

DEGREE = 8
CHUNKS = 2

lowest = -1.0
cutoff = 1.5
ceiling = 4.5
eps_norm = 1e-06

F32 = jnp.float32
BF16 = jnp.bfloat16
VMEM = pl.BlockSpec(memory_space=pltpu.VMEM)
SMEM = pl.BlockSpec(memory_space=pltpu.SMEM)
LIMIT = 10 * 1024 * 1024


def up_to(value, unit):
    return -(-value // unit) * unit


def split(value):
    high = value.astype(BF16)
    return high, (value - high.astype(F32)).astype(BF16)


def mm(left, right):
    return jnp.dot(left, right, preferred_element_type=F32)


def mm_nt(left, right):
    return lax.dot_general(left, right, (((1,), (1,)), ((), ())), preferred_element_type=F32)


def shifted(shard, axis, by):
    count = lax.axis_size(axis)
    pairs = [(i, i + by) for i in range(count) if 0 <= i + by < count]
    return lax.ppermute(shard, axis, pairs)


def coefficients():
    half_width = (ceiling - cutoff) / 2.0
    centre = (ceiling + cutoff) / 2.0
    sigma_one = half_width / (lowest - centre)
    pairs = [(sigma_one / half_width, 0.0)]
    sigma_now = sigma_one
    for _ in range(DEGREE - 1):
        sigma_next = 1.0 / (2.0 / sigma_one - sigma_now)
        pairs.append((2.0 * sigma_next / half_width, sigma_now * sigma_next))
        sigma_now = sigma_next
    return centre, pairs


class Layout:
    def __init__(self, owned, face):
        self.owned = owned
        self.face = face
        self.rest = up_to(owned - face, 8)
        self.fpad = up_to(face, 8)
        self.rows = up_to(self.rest + self.fpad, 16)
        self.ext = up_to(self.rows + self.fpad, 16)
        self.whole = face // 8 * 8
        self.part = face - self.whole

    def packed(self, width):
        lanes = min(width, 128)
        groups = width // lanes
        return groups, lanes, groups * self.whole + up_to(groups * self.part, 8)

    def pack(self, ref, value):
        groups, lanes, _ = self.packed(value.shape[1])
        for group in range(groups):
            columns = value[:, group * lanes : (group + 1) * lanes]
            ref[group * self.whole : (group + 1) * self.whole] = columns[: self.whole]
            at = groups * self.whole + group * self.part
            if self.part:
                ref[at : at + self.part] = columns[self.whole : self.face]
        used = groups * self.face
        if ref.shape[0] > used:
            ref[used:] = jnp.zeros((ref.shape[0] - used, lanes), F32)

    def unpack(self, ref, width):
        groups, lanes, _ = self.packed(width)
        parts = []
        for group in range(groups):
            pieces = [ref[group * self.whole : (group + 1) * self.whole]]
            at = groups * self.whole + group * self.part
            if self.part:
                pieces.append(ref[at : at + self.part])
            pieces.append(jnp.zeros((self.fpad - self.face, lanes), F32))
            parts.append(jnp.concatenate(pieces, axis=0))
        return jnp.concatenate(parts, axis=1) if groups > 1 else parts[0]

    def position(self, ids, faces):
        same = ids[:, None] == faces[None, :]
        slot = jnp.sum(jnp.where(same, jnp.arange(self.face, dtype=jnp.int32)[None, :] + 1, 0), axis=1)
        below = jnp.sum((faces[None, :] < ids[:, None]).astype(jnp.int32), axis=1)
        own = jnp.where(slot > 0, self.rest + slot - 1, ids - below)
        return jnp.where(ids < self.owned, own, self.rows + ids - self.owned)


def arrange_kernel(lay, a_ref, q_ref, bh_ref, bl_ref, gh_ref, gl_ref, corner_ref):
    cells, nodes, _ = a_ref.shape
    total = jnp.zeros((lay.ext, lay.ext), F32)
    for cell in range(cells):
        q = q_ref[cell]
        hot = (lax.broadcasted_iota(jnp.int32, (lay.ext, nodes), 0) == q).astype(F32).astype(BF16)
        for part in split(a_ref[cell]):
            total = total + mm_nt(mm(hot, part).astype(BF16), hot)
    bh_ref[...], bl_ref[...] = split(total[: lay.rows])
    lower = total[lay.rows : lay.rows + lay.fpad]
    gh_ref[...], gl_ref[...] = split(lower[:, : lay.rows])
    corner_ref[...] = lower[:, lay.rows : lay.rows + lay.fpad]


def arrange(lay, matrices, q):
    own = jax.ShapeDtypeStruct((lay.rows, lay.ext), BF16)
    ghost = jax.ShapeDtypeStruct((lay.fpad, lay.rows), BF16)
    return pl.pallas_call(
        lambda *refs: arrange_kernel(lay, *refs),
        out_shape=[own, own, ghost, ghost, jax.ShapeDtypeStruct((lay.fpad, lay.fpad), F32)],
        in_specs=[VMEM, VMEM],
        out_specs=[VMEM] * 5,
        compiler_params=pltpu.CompilerParams(vmem_limit_bytes=LIMIT),
        name="arrange",
    )(matrices, q)


def patch_kernel(lay, corner_ref, high_ref, low_ref, new_high_ref, new_low_ref):
    at = slice(lay.rest, lay.rest + lay.fpad)
    value = high_ref[at, at].astype(F32) + low_ref[at, at].astype(F32) + corner_ref[...]
    new_high_ref[...], new_low_ref[...] = high_ref[...], low_ref[...]
    new_high_ref[at, at], new_low_ref[at, at] = split(value)


def patch(lay, corner, high, low):
    own = jax.ShapeDtypeStruct((lay.rows, lay.ext), BF16)
    return pl.pallas_call(
        lambda *refs: patch_kernel(lay, *refs),
        out_shape=[own, own],
        in_specs=[VMEM] * 3,
        out_specs=[VMEM] * 2,
        compiler_params=pltpu.CompilerParams(vmem_limit_bytes=LIMIT),
        name="patch",
    )(corner, high, low)


def outgoing(lay, odd_ref, gh_ref, gl_ref, value, near_ref, far_ref):
    high, low = split(value)
    gh = gh_ref[...]
    lift = mm(gh, high) + mm(gh, low) + mm(gl_ref[...], high)
    face = value[lay.rest : lay.rest + lay.fpad]
    even = odd_ref[0] == 0
    lay.pack(near_ref, jnp.where(even, lift, face))
    lay.pack(far_ref, jnp.where(even, face, lift))


def rows_of(lay, place_ref):
    ids = lax.broadcasted_iota(jnp.int32, (lay.rows, lay.owned), 0)
    return (ids == place_ref[...]).astype(F32).astype(BF16)


def first_kernel(lay, odd_ref, place_ref, gh_ref, gl_ref, raw_ref, cur_ref, near_ref, far_ref):
    hot = rows_of(lay, place_ref)
    raw = raw_ref[...]
    high, low = split(raw)
    rest = (raw - high.astype(F32) - low.astype(F32)).astype(BF16)
    cur_ref[...] = mm(hot, high) + mm(hot, low) + mm(hot, rest)
    outgoing(lay, odd_ref, gh_ref, gl_ref, cur_ref[...], near_ref, far_ref)


def step_kernel(
    lay, centre, alpha, beta, last, odd_ref, bh_ref, bl_ref, gh_ref, gl_ref, cur_ref, prev_ref, near_ref, far_ref, *outs
):
    new_ref = outs[0]
    high_ref, low_ref = outs[-2:]
    rows, width = cur_ref.shape
    high_ref[:rows], low_ref[:rows] = split(cur_ref[...])
    even = odd_ref[0] == 0
    near, far = lay.unpack(near_ref, width), lay.unpack(far_ref, width)
    ghost, add = jnp.where(even, near, far), jnp.where(even, far, near)
    if lay.ext - rows > lay.fpad:
        ghost = jnp.concatenate([ghost, jnp.zeros((lay.ext - rows - lay.fpad, width), F32)], axis=0)
    high_ref[rows:], low_ref[rows:] = split(ghost)
    block = min(width, 256)

    @pl.loop(0, width // block)
    def _(index):
        columns = pl.ds(pl.multiple_of(index * block, block), block)
        high = high_ref[:, columns]
        value = mm(bh_ref[...], high) + mm(bh_ref[...], low_ref[:, columns]) + mm(bl_ref[...], high)
        new = (value - centre * cur_ref[:, columns]) * alpha
        if beta:
            new = new - beta * prev_ref[:, columns]
        new_ref[:, columns] = new

    new_ref[lay.rest : lay.rest + lay.fpad] += alpha * add
    if last:
        for at, end in ((lay.owned - lay.face, lay.rest), (lay.rest + lay.face, rows)):
            if end > at:
                new_ref[at:end] = jnp.zeros((end - at, width), F32)
    else:
        outgoing(lay, odd_ref, gh_ref, gl_ref, new_ref[...], outs[1], outs[2])


def cost(lay, width):
    return pl.CostEstimate(
        flops=6 * lay.ext * lay.ext * width, bytes_accessed=3 * 4 * lay.rows * width, transcendentals=0
    )


def message(lay, width):
    _, lanes, height = lay.packed(width)
    return jax.ShapeDtypeStruct((height, lanes), F32)


def first(lay, odd, place, gh, gl, raw):
    width = raw.shape[1]
    return pl.pallas_call(
        lambda *refs: first_kernel(lay, *refs),
        out_shape=[jax.ShapeDtypeStruct((lay.rows, width), F32)] + [message(lay, width)] * 2,
        in_specs=[SMEM] + [VMEM] * 4,
        out_specs=[VMEM] * 3,
        compiler_params=pltpu.CompilerParams(vmem_limit_bytes=LIMIT),
        cost_estimate=cost(lay, width),
        name="first",
    )(odd, place, gh, gl, raw)


def advance(lay, centre, alpha, beta, last, odd, matrices, cur, prev, near, far):
    width = cur.shape[1]
    outs = [jax.ShapeDtypeStruct((lay.rows, width), F32)]
    if not last:
        outs += [message(lay, width)] * 2
    return pl.pallas_call(
        lambda *refs: step_kernel(lay, centre, alpha, beta, last, *refs),
        out_shape=outs,
        in_specs=[SMEM] + [VMEM] * 8,
        out_specs=[VMEM] * len(outs),
        scratch_shapes=[pltpu.VMEM((lay.ext, width), BF16)] * 2,
        compiler_params=pltpu.CompilerParams(vmem_limit_bytes=LIMIT),
        cost_estimate=cost(lay, width),
        name="step",
    )(odd, *matrices, cur, prev, near, far)


def neighbours(value, begin):
    count = lax.axis_size("nodes")
    pairs = []
    for low in range(begin, count - 1, 2):
        pairs += [(low, low + 1), (low + 1, low)]
    return lax.ppermute(value, "nodes", pairs)


def filter_chunks(lay, matrices, place, chunks):
    centre, pairs = coefficients()
    odd = (lax.axis_index("nodes") % 2).reshape(1).astype(jnp.int32)
    states = []
    for raw in chunks:
        cur, near, far = first(lay, odd, place, matrices[2], matrices[3], raw)
        states.append((cur, cur, near, far))
    for degree, (alpha, beta) in enumerate(pairs):
        last = degree == len(pairs) - 1
        fresh = []
        for cur, prev, near, far in states:
            near, far = neighbours(near, 0), neighbours(far, 1)
            outs = advance(lay, centre, alpha, beta, last, odd, matrices, cur, prev, near, far)
            fresh.append((outs[0], cur) + tuple(outs[1:]))
        states = fresh
    return [state[0] for state in states]


def inner(left, right):
    return jnp.einsum("no,nq->oq", left, right, precision=lax.Precision.HIGH)


def orthonormalize_ring(filtered, place, owned):
    width = filtered.shape[1]
    total_rows = owned * lax.axis_size("nodes")
    members = lax.axis_size("orb")
    position = lax.axis_index("orb")
    blocks = [filtered]
    for stride in range(1, members // 2 + 1):
        pairs = [(source, (source + stride) % members) for source in range(members)]
        blocks.append(lax.ppermute(filtered, "orb", pairs))
    tiles = lax.psum(jnp.stack([inner(filtered, block) for block in blocks]), "nodes")
    eye = jnp.eye(width, dtype=jnp.bool_)
    diag_own = jnp.sum(jnp.where(eye, tiles[0], 0.0), axis=0)
    diag_all = lax.all_gather(diag_own, "orb", axis=0, tiled=True)
    scale_all = lax.rsqrt(diag_all / total_rows + eps_norm)
    scale_own = lax.rsqrt(diag_own / total_rows + eps_norm)
    unit_own = filtered * scale_own[None, :]
    mixed = jnp.zeros(filtered.shape, F32)
    for stride in range(members // 2 + 1):
        source = (position - stride) % members
        scale_source = lax.dynamic_slice_in_dim(scale_all, source * width, width, 0)
        coupling = tiles[stride] * scale_own[:, None] * scale_source[None, :] / total_rows
        mixed = mixed + jnp.dot(
            blocks[stride] * scale_source[None, :], coupling.T, precision=lax.Precision.HIGH
        )
        if stride > 0 and 2 * stride != members:
            returned = jnp.dot(unit_own, coupling, precision=lax.Precision.HIGH)
            pairs = [(source, (source - stride) % members) for source in range(members)]
            mixed = mixed + lax.ppermute(returned, "orb", pairs)
    rotated = 1.5 * unit_own - 0.5 * mixed
    return rotated[place]


def mm_tn(left, right):
    return lax.dot_general(left, right, (((0,), (0,)), ((), ())), preferred_element_type=F32)


def triple(product, left, right):
    return product(left[0], right[0]) + product(left[0], right[1]) + product(left[1], right[0])


QUARTERS = 4
OWN_BLOCKS = 10
CROSS_BLOCKS = 8
ORDERS = 3


def columns_of(quarter, bs):
    if isinstance(quarter, int):
        return slice(quarter * bs, (quarter + 1) * bs)
    return pl.ds(pl.multiple_of(quarter * bs, bs), bs)


def own_pairs(visit):
    for first, number, ahead in ((0, 4, 0), (4, 4, 1), (8, 2, 2)):
        for row in range(number):
            visit(first + row, row, (row + ahead) % QUARTERS, ahead)


def own_gram_kernel(bs, a_ref, b_ref, out_ref, high_ref, low_ref):
    half = 2 * bs
    high_ref[:, :half], low_ref[:, :half] = split(a_ref[...])
    high_ref[:, half:], low_ref[:, half:] = split(b_ref[...])

    def visit(slot, row, column, ahead):
        left = high_ref[:, columns_of(row, bs)], low_ref[:, columns_of(row, bs)]
        right = high_ref[:, columns_of(column, bs)], low_ref[:, columns_of(column, bs)]
        out_ref[columns_of(slot, bs)] = triple(mm_tn, left, right)

    own_pairs(visit)


def cross_gram_kernel(bs, o_ref, a_ref, b_ref, oa_ref, ob_ref, out_ref, norm_ref, high_ref, low_ref, oh_ref, ol_ref):
    half = 2 * bs
    for index, (ref, high, low) in enumerate(
        ((a_ref, high_ref, low_ref), (b_ref, high_ref, low_ref), (oa_ref, oh_ref, ol_ref), (ob_ref, oh_ref, ol_ref))
    ):
        value = ref[...]
        at = slice(index % 2 * half, (index % 2 + 1) * half)
        high[:, at], low[:, at] = split(value)
        total = jnp.sum(value * value, axis=0, keepdims=True)
        for k in range(2):
            norm_ref[2 * index + k : 2 * index + k + 1] = total[:, k * bs : (k + 1) * bs]
    core = o_ref[0]

    for quarter in range(QUARTERS):
        facing = lax.bitwise_xor(quarter // 2, core)
        left = high_ref[:, columns_of(quarter, bs)], low_ref[:, columns_of(quarter, bs)]
        right = oh_ref[:, columns_of(facing, half)], ol_ref[:, columns_of(facing, half)]
        rows = triple(mm_tn, left, right)
        for k in range(2):
            out_ref[columns_of(2 * quarter + k, bs)] = rows[:, k * bs : (k + 1) * bs]


def own_gram(a, b, bs):
    return pl.pallas_call(
        lambda *refs: own_gram_kernel(bs, *refs),
        out_shape=jax.ShapeDtypeStruct((OWN_BLOCKS * bs, bs), F32),
        in_specs=[VMEM] * 2,
        out_specs=VMEM,
        scratch_shapes=[pltpu.VMEM((a.shape[0], 4 * bs), BF16)] * 2,
        compiler_params=pltpu.CompilerParams(vmem_limit_bytes=LIMIT),
        cost_estimate=pl.CostEstimate(flops=6 * 10 * a.shape[0] * bs * bs, bytes_accessed=4 * a.size, transcendentals=0),
        name="own_gram",
    )(a, b)


def cross_gram(core, a, b, oa, ob, bs):
    return pl.pallas_call(
        lambda *refs: cross_gram_kernel(bs, *refs),
        out_shape=[jax.ShapeDtypeStruct((CROSS_BLOCKS * bs, bs), F32), jax.ShapeDtypeStruct((8, bs), F32)],
        in_specs=[SMEM] + [VMEM] * 4,
        out_specs=[VMEM] * 2,
        scratch_shapes=[pltpu.VMEM((a.shape[0], 4 * bs), BF16)] * 4,
        compiler_params=pltpu.CompilerParams(vmem_limit_bytes=LIMIT),
        cost_estimate=pl.CostEstimate(flops=6 * 8 * a.shape[0] * bs * bs, bytes_accessed=8 * a.size, transcendentals=0),
        name="cross_gram",
    )(core, a, b, oa, ob)


def weigh_kernel(lay, bs, total_rows, norm_ref, place_ref, *refs):
    sources, (wh_ref, wl_ref, back_ref, scale_ref) = refs[:4], refs[4:]
    hot = rows_of(lay, place_ref)
    for quarter in range(2 * QUARTERS):
        scale = lax.rsqrt(norm_ref[quarter : quarter + 1] / total_rows + eps_norm)
        value = sources[quarter // 2][:, quarter % 2 * bs : (quarter % 2 + 1) * bs]
        at = slice(quarter * bs, (quarter + 1) * bs)
        high, low = split(value * (scale * scale * (0.5 / total_rows)))
        wh_ref[:, at], wl_ref[:, at] = mm_tn(hot, high).astype(BF16), mm_tn(hot, low).astype(BF16)
        if quarter < QUARTERS:
            back_ref[:, at] = 1.5 / (scale * scale * (0.5 / total_rows))
            scale_ref[:, at] = scale


def weigh(lay, norms, place, sources, bs, total_rows):
    width = 2 * sources[0].shape[1]
    return pl.pallas_call(
        lambda *refs: weigh_kernel(lay, bs, total_rows, *refs),
        out_shape=[
            jax.ShapeDtypeStruct((lay.owned, 2 * width), BF16),
            jax.ShapeDtypeStruct((lay.owned, 2 * width), BF16),
            jax.ShapeDtypeStruct((1, width), F32),
            jax.ShapeDtypeStruct((1, width), F32),
        ],
        in_specs=[VMEM] * 6,
        out_specs=[VMEM] * 4,
        compiler_params=pltpu.CompilerParams(vmem_limit_bytes=LIMIT),
        cost_estimate=pl.CostEstimate(
            flops=8 * lay.owned * lay.rows * width, bytes_accessed=24 * lay.owned * width, transcendentals=0
        ),
        name="weigh",
    )(norms, place, *sources)


def rotate_own_kernel(bs, wh_ref, wl_ref, back_ref, t_ref, out_ref):
    for quarter in range(QUARTERS):
        at = columns_of(quarter, bs)
        out_ref[:, at] = (wh_ref[:, at].astype(F32) + wl_ref[:, at].astype(F32)) * back_ref[:, at]

    def weight(quarter):
        return wh_ref[:, columns_of(quarter, bs)], wl_ref[:, columns_of(quarter, bs)]

    def visit(slot, row, column, ahead):
        block = split(t_ref[columns_of(slot, bs)])
        out_ref[:, columns_of(column, bs)] -= triple(mm, weight(row), block)
        if ahead:
            out_ref[:, columns_of(row, bs)] -= triple(mm_nt, weight(column), block)

    own_pairs(visit)


def rotate_cross_kernel(bs, o_ref, wh_ref, wl_ref, base_ref, scale_ref, x_ref, p_ref, out_ref):
    core = o_ref[0]

    def weight(quarter):
        return wh_ref[:, columns_of(quarter, bs)], wl_ref[:, columns_of(quarter, bs)]

    @pl.loop(0, QUARTERS)
    def _(j):
        half = lax.shift_right_logical(j, 1)
        inside = lax.bitwise_and(j, 1)
        facing = lax.bitwise_xor(half, core)
        across = 1 - facing
        total = base_ref[:, columns_of(j, bs)]
        for k in range(2):
            mine = split(x_ref[columns_of(half * 4 + inside * 2 + k, bs)])
            total = total - triple(mm_nt, weight(QUARTERS + 2 * facing + k), mine)
            theirs = split(p_ref[columns_of(across * 4 + k * 2 + inside, bs)])
            total = total - triple(mm, weight(QUARTERS + 2 * across + k), theirs)
        out_ref[:, columns_of(j, bs)] = total * scale_ref[:, columns_of(j, bs)]


def rotate_own(wh, wl, back, blocks, bs):
    rows, width = wh.shape[0], back.shape[1]
    return pl.pallas_call(
        lambda *refs: rotate_own_kernel(bs, *refs),
        out_shape=jax.ShapeDtypeStruct((rows, width), F32),
        in_specs=[VMEM] * 4,
        out_specs=VMEM,
        compiler_params=pltpu.CompilerParams(vmem_limit_bytes=LIMIT),
        cost_estimate=pl.CostEstimate(flops=6 * rows * width * width, bytes_accessed=8 * rows * width, transcendentals=0),
        name="rotate_own",
    )(wh, wl, back, blocks)


def rotate_cross(core, wh, wl, base, scale, blocks, partner, bs):
    rows, width = base.shape
    return pl.pallas_call(
        lambda *refs: rotate_cross_kernel(bs, *refs),
        out_shape=jax.ShapeDtypeStruct((rows, width), F32),
        in_specs=[SMEM] + [VMEM] * 6,
        out_specs=VMEM,
        compiler_params=pltpu.CompilerParams(vmem_limit_bytes=LIMIT),
        cost_estimate=pl.CostEstimate(flops=6 * rows * width * width, bytes_accessed=8 * rows * width, transcendentals=0),
        name="rotate_cross",
    )(core, wh, wl, base, scale, blocks, partner)


def exchange(value, axis, bit):
    count = lax.axis_size(axis)
    return lax.ppermute(value, axis, [(i, i ^ (1 << bit)) for i in range(count)])


def side(node, bit):
    return (node >> bit) & 1


class Stream:
    def __init__(self, value, extra=None):
        count = lax.axis_size("nodes")
        self.node = lax.axis_index("nodes")
        bits = list(range(count.bit_length() - 1))
        self.last = bits.pop()
        self.phases = len(bits)
        self.orders = [bits[turn % len(bits) :] + bits[: turn % len(bits)] for turn in range(ORDERS)]
        unit = 8 << self.phases
        units = value.shape[0] // unit
        sizes = [units // ORDERS + (index < units % ORDERS) for index in range(ORDERS)]
        self.values, at = [], 0
        for size in sizes:
            self.values.append(value[at : at + size * unit])
            at += size * unit
        self.extra = extra

    def scatter_start(self, phase):
        self.kept, away = [], []
        for value, order in zip(self.values, self.orders):
            half = value.shape[0] // 2
            mine = side(self.node, order[phase]) * half
            self.kept.append(lax.dynamic_slice_in_dim(value, mine, half, 0))
            away.append(lax.dynamic_slice_in_dim(value, half - mine, half, 0))
        if self.extra is not None:
            away[-1] = jnp.concatenate([away[-1], self.extra], axis=0)
        self.got = [exchange(value, "nodes", order[phase]) for value, order in zip(away, self.orders)]

    def scatter_done(self):
        self.got = lax.optimization_barrier(self.got)
        if self.extra is not None:
            half = self.kept[-1].shape[0]
            self.extra = self.extra + self.got[-1][half:]
            self.got[-1] = self.got[-1][:half]
        self.values = [keep + value for keep, value in zip(self.kept, self.got)]

    def middle_start(self):
        parts = self.values + ([self.extra] if self.extra is not None else [])
        self.whole = jnp.concatenate(parts, axis=0)
        self.got = exchange(self.whole, "nodes", self.last)

    def middle_done(self):
        total, at, parts = self.whole + self.got, 0, []
        for value in self.values:
            parts.append(total[at : at + value.shape[0]])
            at += value.shape[0]
        self.values = parts
        if self.extra is not None:
            self.extra = total[at:]

    def gather_start(self, phase):
        self.got = [exchange(value, "nodes", order[phase]) for value, order in zip(self.values, self.orders)]
        self.phase = phase

    def gather_done(self):
        self.got = lax.optimization_barrier(self.got)
        values = []
        for value, got, order in zip(self.values, self.got, self.orders):
            lower = side(self.node, order[self.phase]) == 0
            values += [jnp.where(lower, value, got), jnp.where(lower, got, value)]
        if self.phase == 0:
            self.values = [jnp.concatenate(values, axis=0)]
        else:
            self.values = [jnp.concatenate(values[2 * i : 2 * i + 2], axis=0) for i in range(ORDERS)]


def orthonormalize_pair(lay, a, b, place, bs):
    core = lax.axis_index("orb")
    index = core.reshape(1).astype(jnp.int32)
    oa, ob = exchange(a, "orb", 0), exchange(b, "orb", 0)
    own = Stream(own_gram(a, b, bs))
    own.scatter_start(0)
    blocks, norms = cross_gram(index, a, b, oa, ob, bs)
    own.got, blocks, norms = lax.optimization_barrier((own.got, blocks, norms))
    cross = Stream(blocks, norms)
    cross.scatter_start(0)
    own.scatter_done()
    for phase in range(1, own.phases):
        own.scatter_start(phase)
        cross.scatter_done()
        cross.scatter_start(phase)
        own.scatter_done()
    own.middle_start()
    cross.scatter_done()
    cross.middle_start()
    own.middle_done()
    together = lax.optimization_barrier
    for phase in reversed(range(own.phases)):
        own.gather_start(phase)
        if phase == own.phases - 1:
            cross.middle_done()
        else:
            cross.gather_done()
        if phase == 0:
            weights = weigh(
                lay, cross.extra, place, (a, b, oa, ob), bs, lay.owned * lax.axis_size("nodes")
            )
            own.got, (wh, wl, back, scale) = together((own.got, weights))
        cross.gather_start(phase)
        own.gather_done()
    base = rotate_own(wh, wl, back, own.values[0], bs)
    cross.got, base = together((cross.got, base))
    cross.gather_done()
    partner = exchange(cross.values[0], "orb", 0)
    return rotate_cross(index, wh, wl, base, scale, cross.values[0], partner, bs)


def body(orbitals, cell_matrix, connectivity, face_nodes):
    owned, width = orbitals.shape
    lay = Layout(owned, face_nodes.shape[0])
    cells, nodes = connectivity.shape
    place = lay.position(jnp.arange(owned, dtype=jnp.int32), face_nodes)
    q = lay.position(connectivity.reshape(-1), face_nodes).reshape(cells, 1, nodes)
    spot = place.reshape(1, owned)
    bh, bl, gh, gl, corner = arrange(lay, cell_matrix, q)
    matrices = (*patch(lay, shifted(corner, "nodes", 1), bh, bl), gh, gl)

    step = width // CHUNKS
    parts = filter_chunks(lay, matrices, spot, [orbitals[:, i * step : (i + 1) * step] for i in range(CHUNKS)])
    count = lax.axis_size("nodes")
    bs = width // QUARTERS
    if lax.axis_size("orb") == 2 and CHUNKS == 2 and count & (count - 1) == 0 and count > 2 and bs % 128 == 0 and 2 * bs % (4 * count) == 0:
        return orthonormalize_pair(lay, parts[0], parts[1], spot, bs)
    return orthonormalize_ring(jnp.concatenate(parts, axis=1), place, owned)


def solution(mesh):
    return jax.shard_map(
        body,
        mesh=mesh,
        in_specs=(P("nodes", "orb"), P("nodes", None, None), P("nodes", None), P("nodes")),
        out_specs=P("nodes", "orb"),
        check_vma=False,
    )
```

```python
import jax
import jax.numpy as jnp
from jax import lax
from jax.experimental import pallas as pl
from jax.experimental.pallas import tpu as pltpu
from jax.sharding import PartitionSpec as P

DEGREE = 8
CHUNKS = 2

lowest = -1.0
cutoff = 1.5
ceiling = 4.5
eps_norm = 1e-06

F32 = jnp.float32
BF16 = jnp.bfloat16
VMEM = pl.BlockSpec(memory_space=pltpu.VMEM)
SMEM = pl.BlockSpec(memory_space=pltpu.SMEM)
LIMIT = 10 * 1024 * 1024


def up_to(value, unit):
    return -(-value // unit) * unit


def split(value):
    high = value.astype(BF16)
    return high, (value - high.astype(F32)).astype(BF16)


def mm(left, right):
    return jnp.dot(left, right, preferred_element_type=F32)


def mm_nt(left, right):
    return lax.dot_general(left, right, (((1,), (1,)), ((), ())), preferred_element_type=F32)


def shifted(shard, axis, by):
    count = lax.axis_size(axis)
    pairs = [(i, i + by) for i in range(count) if 0 <= i + by < count]
    return lax.ppermute(shard, axis, pairs)


def coefficients():
    half_width = (ceiling - cutoff) / 2.0
    centre = (ceiling + cutoff) / 2.0
    sigma_one = half_width / (lowest - centre)
    pairs = [(sigma_one / half_width, 0.0)]
    sigma_now = sigma_one
    for _ in range(DEGREE - 1):
        sigma_next = 1.0 / (2.0 / sigma_one - sigma_now)
        pairs.append((2.0 * sigma_next / half_width, sigma_now * sigma_next))
        sigma_now = sigma_next
    return centre, pairs


class Layout:
    def __init__(self, owned, face):
        self.owned = owned
        self.face = face
        self.rest = up_to(owned - face, 8)
        self.fpad = up_to(face, 8)
        self.rows = up_to(self.rest + self.fpad, 16)
        self.ext = up_to(self.rows + self.fpad, 16)
        self.whole = face // 8 * 8
        self.part = face - self.whole

    def packed(self, width):
        lanes = min(width, 128)
        groups = width // lanes
        return groups, lanes, groups * self.whole + up_to(groups * self.part, 8)

    def pack(self, ref, value):
        groups, lanes, _ = self.packed(value.shape[1])
        for group in range(groups):
            columns = value[:, group * lanes : (group + 1) * lanes]
            ref[group * self.whole : (group + 1) * self.whole] = columns[: self.whole]
            at = groups * self.whole + group * self.part
            if self.part:
                ref[at : at + self.part] = columns[self.whole : self.face]
        used = groups * self.face
        if ref.shape[0] > used:
            ref[used:] = jnp.zeros((ref.shape[0] - used, lanes), F32)

    def unpack(self, ref, width):
        groups, lanes, _ = self.packed(width)
        parts = []
        for group in range(groups):
            pieces = [ref[group * self.whole : (group + 1) * self.whole]]
            at = groups * self.whole + group * self.part
            if self.part:
                pieces.append(ref[at : at + self.part])
            pieces.append(jnp.zeros((self.fpad - self.face, lanes), F32))
            parts.append(jnp.concatenate(pieces, axis=0))
        return jnp.concatenate(parts, axis=1) if groups > 1 else parts[0]

    def position(self, ids, faces):
        same = ids[:, None] == faces[None, :]
        slot = jnp.sum(jnp.where(same, jnp.arange(self.face, dtype=jnp.int32)[None, :] + 1, 0), axis=1)
        below = jnp.sum((faces[None, :] < ids[:, None]).astype(jnp.int32), axis=1)
        own = jnp.where(slot > 0, self.rest + slot - 1, ids - below)
        return jnp.where(ids < self.owned, own, self.rows + ids - self.owned)


def arrange_kernel(lay, a_ref, q_ref, bh_ref, bl_ref, gh_ref, gl_ref, corner_ref):
    cells, nodes, _ = a_ref.shape
    total = jnp.zeros((lay.ext, lay.ext), F32)
    for cell in range(cells):
        q = q_ref[cell]
        hot = (lax.broadcasted_iota(jnp.int32, (lay.ext, nodes), 0) == q).astype(F32).astype(BF16)
        for part in split(a_ref[cell]):
            total = total + mm_nt(mm(hot, part).astype(BF16), hot)
    bh_ref[...], bl_ref[...] = split(total[: lay.rows])
    lower = total[lay.rows : lay.rows + lay.fpad]
    gh_ref[...], gl_ref[...] = split(lower[:, : lay.rows])
    corner_ref[...] = lower[:, lay.rows : lay.rows + lay.fpad]


def arrange(lay, matrices, q):
    own = jax.ShapeDtypeStruct((lay.rows, lay.ext), BF16)
    ghost = jax.ShapeDtypeStruct((lay.fpad, lay.rows), BF16)
    return pl.pallas_call(
        lambda *refs: arrange_kernel(lay, *refs),
        out_shape=[own, own, ghost, ghost, jax.ShapeDtypeStruct((lay.fpad, lay.fpad), F32)],
        in_specs=[VMEM, VMEM],
        out_specs=[VMEM] * 5,
        compiler_params=pltpu.CompilerParams(vmem_limit_bytes=LIMIT),
        name="arrange",
    )(matrices, q)


def patch_kernel(lay, corner_ref, high_ref, low_ref, new_high_ref, new_low_ref):
    at = slice(lay.rest, lay.rest + lay.fpad)
    value = high_ref[at, at].astype(F32) + low_ref[at, at].astype(F32) + corner_ref[...]
    new_high_ref[...], new_low_ref[...] = high_ref[...], low_ref[...]
    new_high_ref[at, at], new_low_ref[at, at] = split(value)


def patch(lay, corner, high, low):
    own = jax.ShapeDtypeStruct((lay.rows, lay.ext), BF16)
    return pl.pallas_call(
        lambda *refs: patch_kernel(lay, *refs),
        out_shape=[own, own],
        in_specs=[VMEM] * 3,
        out_specs=[VMEM] * 2,
        compiler_params=pltpu.CompilerParams(vmem_limit_bytes=LIMIT),
        name="patch",
    )(corner, high, low)


def outgoing(lay, odd_ref, gh_ref, gl_ref, value, near_ref, far_ref):
    high, low = split(value)
    gh = gh_ref[...]
    lift = mm(gh, high) + mm(gh, low) + mm(gl_ref[...], high)
    face = value[lay.rest : lay.rest + lay.fpad]
    even = odd_ref[0] == 0
    lay.pack(near_ref, jnp.where(even, lift, face))
    lay.pack(far_ref, jnp.where(even, face, lift))


def rows_of(lay, place_ref):
    ids = lax.broadcasted_iota(jnp.int32, (lay.rows, lay.owned), 0)
    return (ids == place_ref[...]).astype(F32).astype(BF16)


def first_kernel(lay, odd_ref, place_ref, gh_ref, gl_ref, raw_ref, cur_ref, near_ref, far_ref):
    hot = rows_of(lay, place_ref)
    raw = raw_ref[...]
    high, low = split(raw)
    rest = (raw - high.astype(F32) - low.astype(F32)).astype(BF16)
    cur_ref[...] = mm(hot, high) + mm(hot, low) + mm(hot, rest)
    outgoing(lay, odd_ref, gh_ref, gl_ref, cur_ref[...], near_ref, far_ref)


def step_kernel(
    lay, centre, alpha, beta, last, odd_ref, bh_ref, bl_ref, gh_ref, gl_ref, cur_ref, prev_ref, near_ref, far_ref, *outs
):
    new_ref = outs[0]
    high_ref, low_ref = outs[-2:]
    rows, width = cur_ref.shape
    high_ref[:rows], low_ref[:rows] = split(cur_ref[...])
    even = odd_ref[0] == 0
    near, far = lay.unpack(near_ref, width), lay.unpack(far_ref, width)
    ghost, add = jnp.where(even, near, far), jnp.where(even, far, near)
    if lay.ext - rows > lay.fpad:
        ghost = jnp.concatenate([ghost, jnp.zeros((lay.ext - rows - lay.fpad, width), F32)], axis=0)
    high_ref[rows:], low_ref[rows:] = split(ghost)
    block = min(width, 256)

    @pl.loop(0, width // block)
    def _(index):
        columns = pl.ds(pl.multiple_of(index * block, block), block)
        high = high_ref[:, columns]
        value = mm(bh_ref[...], high) + mm(bh_ref[...], low_ref[:, columns]) + mm(bl_ref[...], high)
        new = (value - centre * cur_ref[:, columns]) * alpha
        if beta:
            new = new - beta * prev_ref[:, columns]
        new_ref[:, columns] = new

    new_ref[lay.rest : lay.rest + lay.fpad] += alpha * add
    if last:
        for at, end in ((lay.owned - lay.face, lay.rest), (lay.rest + lay.face, rows)):
            if end > at:
                new_ref[at:end] = jnp.zeros((end - at, width), F32)
    else:
        outgoing(lay, odd_ref, gh_ref, gl_ref, new_ref[...], outs[1], outs[2])


def cost(lay, width):
    return pl.CostEstimate(
        flops=6 * lay.ext * lay.ext * width, bytes_accessed=3 * 4 * lay.rows * width, transcendentals=0
    )


def message(lay, width):
    _, lanes, height = lay.packed(width)
    return jax.ShapeDtypeStruct((height, lanes), F32)


def first(lay, odd, place, gh, gl, raw):
    width = raw.shape[1]
    return pl.pallas_call(
        lambda *refs: first_kernel(lay, *refs),
        out_shape=[jax.ShapeDtypeStruct((lay.rows, width), F32)] + [message(lay, width)] * 2,
        in_specs=[SMEM] + [VMEM] * 4,
        out_specs=[VMEM] * 3,
        compiler_params=pltpu.CompilerParams(vmem_limit_bytes=LIMIT),
        cost_estimate=cost(lay, width),
        name="first",
    )(odd, place, gh, gl, raw)


def advance(lay, centre, alpha, beta, last, odd, matrices, cur, prev, near, far):
    width = cur.shape[1]
    outs = [jax.ShapeDtypeStruct((lay.rows, width), F32)]
    if not last:
        outs += [message(lay, width)] * 2
    return pl.pallas_call(
        lambda *refs: step_kernel(lay, centre, alpha, beta, last, *refs),
        out_shape=outs,
        in_specs=[SMEM] + [VMEM] * 8,
        out_specs=[VMEM] * len(outs),
        scratch_shapes=[pltpu.VMEM((lay.ext, width), BF16)] * 2,
        compiler_params=pltpu.CompilerParams(vmem_limit_bytes=LIMIT),
        cost_estimate=cost(lay, width),
        name="step",
    )(odd, *matrices, cur, prev, near, far)


def neighbours(value, begin):
    count = lax.axis_size("nodes")
    pairs = []
    for low in range(begin, count - 1, 2):
        pairs += [(low, low + 1), (low + 1, low)]
    return lax.ppermute(value, "nodes", pairs)


def filter_chunks(lay, matrices, place, chunks):
    centre, pairs = coefficients()
    odd = (lax.axis_index("nodes") % 2).reshape(1).astype(jnp.int32)
    states = []
    for raw in chunks:
        cur, near, far = first(lay, odd, place, matrices[2], matrices[3], raw)
        states.append((cur, cur, near, far))
    for degree, (alpha, beta) in enumerate(pairs):
        last = degree == len(pairs) - 1
        fresh = []
        for cur, prev, near, far in states:
            near, far = neighbours(near, 0), neighbours(far, 1)
            outs = advance(lay, centre, alpha, beta, last, odd, matrices, cur, prev, near, far)
            fresh.append((outs[0], cur) + tuple(outs[1:]))
        states = fresh
    return [state[0] for state in states]


def inner(left, right):
    return jnp.einsum("no,nq->oq", left, right, precision=lax.Precision.HIGH)


def orthonormalize_ring(filtered, place, owned):
    width = filtered.shape[1]
    total_rows = owned * lax.axis_size("nodes")
    members = lax.axis_size("orb")
    position = lax.axis_index("orb")
    blocks = [filtered]
    for stride in range(1, members // 2 + 1):
        pairs = [(source, (source + stride) % members) for source in range(members)]
        blocks.append(lax.ppermute(filtered, "orb", pairs))
    tiles = lax.psum(jnp.stack([inner(filtered, block) for block in blocks]), "nodes")
    eye = jnp.eye(width, dtype=jnp.bool_)
    diag_own = jnp.sum(jnp.where(eye, tiles[0], 0.0), axis=0)
    diag_all = lax.all_gather(diag_own, "orb", axis=0, tiled=True)
    scale_all = lax.rsqrt(diag_all / total_rows + eps_norm)
    scale_own = lax.rsqrt(diag_own / total_rows + eps_norm)
    unit_own = filtered * scale_own[None, :]
    mixed = jnp.zeros(filtered.shape, F32)
    for stride in range(members // 2 + 1):
        source = (position - stride) % members
        scale_source = lax.dynamic_slice_in_dim(scale_all, source * width, width, 0)
        coupling = tiles[stride] * scale_own[:, None] * scale_source[None, :] / total_rows
        mixed = mixed + jnp.dot(
            blocks[stride] * scale_source[None, :], coupling.T, precision=lax.Precision.HIGH
        )
        if stride > 0 and 2 * stride != members:
            returned = jnp.dot(unit_own, coupling, precision=lax.Precision.HIGH)
            pairs = [(source, (source - stride) % members) for source in range(members)]
            mixed = mixed + lax.ppermute(returned, "orb", pairs)
    rotated = 1.5 * unit_own - 0.5 * mixed
    return rotated[place]


def mm_tn(left, right):
    return lax.dot_general(left, right, (((0,), (0,)), ((), ())), preferred_element_type=F32)


def triple(product, left, right):
    return product(left[0], right[0]) + product(left[0], right[1]) + product(left[1], right[0])


QUARTERS = 4
OWN_BLOCKS = 10
CROSS_BLOCKS = 8
ORDERS = 3


def columns_of(quarter, bs):
    if isinstance(quarter, int):
        return slice(quarter * bs, (quarter + 1) * bs)
    return pl.ds(pl.multiple_of(quarter * bs, bs), bs)


def own_pairs(visit):
    for first, number, ahead in ((0, 4, 0), (4, 4, 1), (8, 2, 2)):
        for row in range(number):
            visit(first + row, row, (row + ahead) % QUARTERS, ahead)


def own_gram_kernel(bs, a_ref, b_ref, out_ref, high_ref, low_ref):
    half = 2 * bs
    high_ref[:, :half], low_ref[:, :half] = split(a_ref[...])
    high_ref[:, half:], low_ref[:, half:] = split(b_ref[...])

    def visit(slot, row, column, ahead):
        left = high_ref[:, columns_of(row, bs)], low_ref[:, columns_of(row, bs)]
        right = high_ref[:, columns_of(column, bs)], low_ref[:, columns_of(column, bs)]
        out_ref[columns_of(slot, bs)] = triple(mm_tn, left, right)

    own_pairs(visit)


def cross_gram_kernel(bs, o_ref, a_ref, b_ref, oa_ref, ob_ref, out_ref, norm_ref, high_ref, low_ref, oh_ref, ol_ref):
    half = 2 * bs
    for index, (ref, high, low) in enumerate(
        ((a_ref, high_ref, low_ref), (b_ref, high_ref, low_ref), (oa_ref, oh_ref, ol_ref), (ob_ref, oh_ref, ol_ref))
    ):
        value = ref[...]
        at = slice(index % 2 * half, (index % 2 + 1) * half)
        high[:, at], low[:, at] = split(value)
        total = jnp.sum(value * value, axis=0, keepdims=True)
        for k in range(2):
            norm_ref[2 * index + k : 2 * index + k + 1] = total[:, k * bs : (k + 1) * bs]
    core = o_ref[0]

    for quarter in range(QUARTERS):
        facing = lax.bitwise_xor(quarter // 2, core)
        left = high_ref[:, columns_of(quarter, bs)], low_ref[:, columns_of(quarter, bs)]
        right = oh_ref[:, columns_of(facing, half)], ol_ref[:, columns_of(facing, half)]
        rows = triple(mm_tn, left, right)
        for k in range(2):
            out_ref[columns_of(2 * quarter + k, bs)] = rows[:, k * bs : (k + 1) * bs]


def own_gram(a, b, bs):
    return pl.pallas_call(
        lambda *refs: own_gram_kernel(bs, *refs),
        out_shape=jax.ShapeDtypeStruct((OWN_BLOCKS * bs, bs), F32),
        in_specs=[VMEM] * 2,
        out_specs=VMEM,
        scratch_shapes=[pltpu.VMEM((a.shape[0], 4 * bs), BF16)] * 2,
        compiler_params=pltpu.CompilerParams(vmem_limit_bytes=LIMIT),
        cost_estimate=pl.CostEstimate(flops=6 * 10 * a.shape[0] * bs * bs, bytes_accessed=4 * a.size, transcendentals=0),
        name="own_gram",
    )(a, b)


def cross_gram(core, a, b, oa, ob, bs):
    return pl.pallas_call(
        lambda *refs: cross_gram_kernel(bs, *refs),
        out_shape=[jax.ShapeDtypeStruct((CROSS_BLOCKS * bs, bs), F32), jax.ShapeDtypeStruct((8, bs), F32)],
        in_specs=[SMEM] + [VMEM] * 4,
        out_specs=[VMEM] * 2,
        scratch_shapes=[pltpu.VMEM((a.shape[0], 4 * bs), BF16)] * 4,
        compiler_params=pltpu.CompilerParams(vmem_limit_bytes=LIMIT),
        cost_estimate=pl.CostEstimate(flops=6 * 8 * a.shape[0] * bs * bs, bytes_accessed=8 * a.size, transcendentals=0),
        name="cross_gram",
    )(core, a, b, oa, ob)


def weigh_kernel(lay, bs, total_rows, norm_ref, place_ref, *refs):
    sources, (wh_ref, wl_ref, back_ref, scale_ref) = refs[:4], refs[4:]
    hot = rows_of(lay, place_ref)
    for quarter in range(2 * QUARTERS):
        scale = lax.rsqrt(norm_ref[quarter : quarter + 1] / total_rows + eps_norm)
        value = sources[quarter // 2][:, quarter % 2 * bs : (quarter % 2 + 1) * bs]
        at = slice(quarter * bs, (quarter + 1) * bs)
        high, low = split(value * (scale * scale * (0.5 / total_rows)))
        wh_ref[:, at], wl_ref[:, at] = mm_tn(hot, high).astype(BF16), mm_tn(hot, low).astype(BF16)
        if quarter < QUARTERS:
            back_ref[:, at] = 1.5 / (scale * scale * (0.5 / total_rows))
            scale_ref[:, at] = scale


def weigh(lay, norms, place, sources, bs, total_rows):
    width = 2 * sources[0].shape[1]
    return pl.pallas_call(
        lambda *refs: weigh_kernel(lay, bs, total_rows, *refs),
        out_shape=[
            jax.ShapeDtypeStruct((lay.owned, 2 * width), BF16),
            jax.ShapeDtypeStruct((lay.owned, 2 * width), BF16),
            jax.ShapeDtypeStruct((1, width), F32),
            jax.ShapeDtypeStruct((1, width), F32),
        ],
        in_specs=[VMEM] * 6,
        out_specs=[VMEM] * 4,
        compiler_params=pltpu.CompilerParams(vmem_limit_bytes=LIMIT),
        cost_estimate=pl.CostEstimate(
            flops=8 * lay.owned * lay.rows * width, bytes_accessed=24 * lay.owned * width, transcendentals=0
        ),
        name="weigh",
    )(norms, place, *sources)


def rotate_own_kernel(bs, wh_ref, wl_ref, back_ref, t_ref, out_ref):
    for quarter in range(QUARTERS):
        at = columns_of(quarter, bs)
        out_ref[:, at] = (wh_ref[:, at].astype(F32) + wl_ref[:, at].astype(F32)) * back_ref[:, at]

    def weight(quarter):
        return wh_ref[:, columns_of(quarter, bs)], wl_ref[:, columns_of(quarter, bs)]

    def visit(slot, row, column, ahead):
        block = split(t_ref[columns_of(slot, bs)])
        out_ref[:, columns_of(column, bs)] -= triple(mm, weight(row), block)
        if ahead:
            out_ref[:, columns_of(row, bs)] -= triple(mm_nt, weight(column), block)

    own_pairs(visit)


def rotate_cross_kernel(bs, o_ref, wh_ref, wl_ref, base_ref, scale_ref, x_ref, p_ref, out_ref):
    core = o_ref[0]

    def weight(quarter):
        return wh_ref[:, columns_of(quarter, bs)], wl_ref[:, columns_of(quarter, bs)]

    @pl.loop(0, QUARTERS)
    def _(j):
        half = lax.shift_right_logical(j, 1)
        inside = lax.bitwise_and(j, 1)
        facing = lax.bitwise_xor(half, core)
        across = 1 - facing
        total = base_ref[:, columns_of(j, bs)]
        for k in range(2):
            mine = split(x_ref[columns_of(half * 4 + inside * 2 + k, bs)])
            total = total - triple(mm_nt, weight(QUARTERS + 2 * facing + k), mine)
            theirs = split(p_ref[columns_of(across * 4 + k * 2 + inside, bs)])
            total = total - triple(mm, weight(QUARTERS + 2 * across + k), theirs)
        out_ref[:, columns_of(j, bs)] = total * scale_ref[:, columns_of(j, bs)]


def rotate_own(wh, wl, back, blocks, bs):
    rows, width = wh.shape[0], back.shape[1]
    return pl.pallas_call(
        lambda *refs: rotate_own_kernel(bs, *refs),
        out_shape=jax.ShapeDtypeStruct((rows, width), F32),
        in_specs=[VMEM] * 4,
        out_specs=VMEM,
        compiler_params=pltpu.CompilerParams(vmem_limit_bytes=LIMIT),
        cost_estimate=pl.CostEstimate(flops=6 * rows * width * width, bytes_accessed=8 * rows * width, transcendentals=0),
        name="rotate_own",
    )(wh, wl, back, blocks)


def rotate_cross(core, wh, wl, base, scale, blocks, partner, bs):
    rows, width = base.shape
    return pl.pallas_call(
        lambda *refs: rotate_cross_kernel(bs, *refs),
        out_shape=jax.ShapeDtypeStruct((rows, width), F32),
        in_specs=[SMEM] + [VMEM] * 6,
        out_specs=VMEM,
        compiler_params=pltpu.CompilerParams(vmem_limit_bytes=LIMIT),
        cost_estimate=pl.CostEstimate(flops=6 * rows * width * width, bytes_accessed=8 * rows * width, transcendentals=0),
        name="rotate_cross",
    )(core, wh, wl, base, scale, blocks, partner)


def exchange(value, axis, bit):
    count = lax.axis_size(axis)
    return lax.ppermute(value, axis, [(i, i ^ (1 << bit)) for i in range(count)])


def side(node, bit):
    return (node >> bit) & 1


def fold_kernel(summed, carries, whole, *refs):
    refs = list(refs)
    sides_ref = None if whole else refs.pop(0)
    keeps, refs = refs[:ORDERS], refs[ORDERS:]
    gots = [None] * ORDERS
    if summed:
        gots, refs = refs[:ORDERS], refs[ORDERS:]
    norms = None
    if carries:
        norm_ref, refs = refs[0], refs[1:]
        norms = norm_ref[...]
        if summed:
            norms = norms + gots[-1][keeps[-1].shape[0] :]

    def rows(index, at):
        value = keeps[index][at]
        return value + gots[index][at] if summed else value

    if whole:
        at = 0
        for index in range(ORDERS):
            size = keeps[index].shape[0]
            refs[0][at : at + size] = rows(index, slice(0, size))
            at += size
        if carries:
            refs[0][at:] = norms
        return
    aways, kept = refs[:ORDERS], refs[ORDERS : 2 * ORDERS]
    for index in range(ORDERS):
        half = kept[index].shape[0]
        mine = pl.multiple_of(sides_ref[index] * half, 8)
        theirs = pl.multiple_of((1 - sides_ref[index]) * half, 8)
        aways[index][:half] = rows(index, pl.ds(theirs, half))
        kept[index][...] = rows(index, pl.ds(mine, half))
    if carries:
        aways[-1][kept[-1].shape[0] :] = norms
        refs[2 * ORDERS][...] = norms


def fold(sides, keeps, gots, norms, whole):
    columns = keeps[0].shape[1]
    extra = 0 if norms is None else norms.shape[0]
    shape = lambda size: jax.ShapeDtypeStruct((size, columns), F32)
    if whole:
        outs = [shape(sum(keep.shape[0] for keep in keeps) + extra)]
    else:
        halves = [keep.shape[0] // 2 for keep in keeps]
        outs = [shape(half) for half in halves[:-1]] + [shape(halves[-1] + extra)]
        outs += [shape(half) for half in halves] + ([shape(extra)] if extra else [])
    operands = keeps + (gots or []) + ([norms] if extra else [])
    return pl.pallas_call(
        lambda *refs: fold_kernel(bool(gots), bool(extra), whole, *refs),
        out_shape=outs,
        in_specs=([] if whole else [SMEM]) + [VMEM] * len(operands),
        out_specs=[VMEM] * len(outs),
        compiler_params=pltpu.CompilerParams(vmem_limit_bytes=LIMIT),
        cost_estimate=pl.CostEstimate(flops=keeps[0].size, bytes_accessed=24 * keeps[0].size, transcendentals=0),
        name="fold",
    )(*([] if whole else [sides]), *operands)


class Stream:
    def __init__(self, value, extra=None):
        count = lax.axis_size("nodes")
        self.node = lax.axis_index("nodes").astype(jnp.int32)
        bits = list(range(count.bit_length() - 1))
        self.last = bits.pop()
        self.phases = len(bits)
        self.orders = [bits[turn % len(bits) :] + bits[: turn % len(bits)] for turn in range(ORDERS)]
        unit = 8 << self.phases
        units = value.shape[0] // unit
        sizes = [units // ORDERS + (index < units % ORDERS) for index in range(ORDERS)]
        self.values, at = [], 0
        for size in sizes:
            self.values.append(value[at : at + size * unit])
            at += size * unit
        self.extra = extra
        self.got = None

    def scatter_start(self, phase):
        sides = jnp.stack([side(self.node, order[phase]) for order in self.orders])
        outs = fold(sides, self.values, self.got, self.extra, False)
        self.values = list(outs[ORDERS : 2 * ORDERS])
        if self.extra is not None:
            self.extra = outs[2 * ORDERS]
        self.got = [exchange(value, "nodes", order[phase]) for value, order in zip(outs, self.orders)]

    def middle_start(self):
        self.whole = fold(None, self.values, self.got, self.extra, True)[0]
        self.got = exchange(self.whole, "nodes", self.last)

    def middle_done(self):
        total, at, parts = self.whole + self.got, 0, []
        for value in self.values:
            parts.append(total[at : at + value.shape[0]])
            at += value.shape[0]
        self.values = parts
        if self.extra is not None:
            self.extra = total[at:]

    def gather_start(self, phase):
        self.got = [exchange(value, "nodes", order[phase]) for value, order in zip(self.values, self.orders)]
        self.phase = phase

    def gather_done(self):
        self.got = lax.optimization_barrier(self.got)
        values = []
        for value, got, order in zip(self.values, self.got, self.orders):
            lower = side(self.node, order[self.phase]) == 0
            values += [jnp.where(lower, value, got), jnp.where(lower, got, value)]
        if self.phase == 0:
            self.values = [jnp.concatenate(values, axis=0)]
        else:
            self.values = [jnp.concatenate(values[2 * i : 2 * i + 2], axis=0) for i in range(ORDERS)]


def orthonormalize_pair(lay, a, b, place, bs):
    core = lax.axis_index("orb")
    index = core.reshape(1).astype(jnp.int32)
    oa, ob = exchange(a, "orb", 0), exchange(b, "orb", 0)
    own = Stream(own_gram(a, b, bs))
    own.scatter_start(0)
    blocks, norms = cross_gram(index, a, b, oa, ob, bs)
    own.got, blocks, norms = lax.optimization_barrier((own.got, blocks, norms))
    cross = Stream(blocks, norms)
    cross.scatter_start(0)
    for phase in range(1, own.phases):
        own.scatter_start(phase)
        cross.scatter_start(phase)
    own.middle_start()
    cross.middle_start()
    own.middle_done()
    together = lax.optimization_barrier
    for phase in reversed(range(own.phases)):
        own.gather_start(phase)
        if phase == own.phases - 1:
            cross.middle_done()
        else:
            cross.gather_done()
        if phase == 0:
            weights = weigh(
                lay, cross.extra, place, (a, b, oa, ob), bs, lay.owned * lax.axis_size("nodes")
            )
            own.got, (wh, wl, back, scale) = together((own.got, weights))
        cross.gather_start(phase)
        own.gather_done()
    base = rotate_own(wh, wl, back, own.values[0], bs)
    cross.got, base = together((cross.got, base))
    cross.gather_done()
    partner = exchange(cross.values[0], "orb", 0)
    return rotate_cross(index, wh, wl, base, scale, cross.values[0], partner, bs)


def body(orbitals, cell_matrix, connectivity, face_nodes):
    owned, width = orbitals.shape
    lay = Layout(owned, face_nodes.shape[0])
    cells, nodes = connectivity.shape
    place = lay.position(jnp.arange(owned, dtype=jnp.int32), face_nodes)
    q = lay.position(connectivity.reshape(-1), face_nodes).reshape(cells, 1, nodes)
    spot = place.reshape(1, owned)
    bh, bl, gh, gl, corner = arrange(lay, cell_matrix, q)
    matrices = (*patch(lay, shifted(corner, "nodes", 1), bh, bl), gh, gl)

    step = width // CHUNKS
    parts = filter_chunks(lay, matrices, spot, [orbitals[:, i * step : (i + 1) * step] for i in range(CHUNKS)])
    count = lax.axis_size("nodes")
    bs = width // QUARTERS
    if lax.axis_size("orb") == 2 and CHUNKS == 2 and count & (count - 1) == 0 and count > 2 and bs % 128 == 0 and 2 * bs % (4 * count) == 0:
        return orthonormalize_pair(lay, parts[0], parts[1], spot, bs)
    return orthonormalize_ring(jnp.concatenate(parts, axis=1), place, owned)


def solution(mesh):
    return jax.shard_map(
        body,
        mesh=mesh,
        in_specs=(P("nodes", "orb"), P("nodes", None, None), P("nodes", None), P("nodes")),
        out_specs=P("nodes", "orb"),
        check_vma=False,
    )
```

```python
import jax
import jax.numpy as jnp
from jax import lax
from jax.experimental import pallas as pl
from jax.experimental.pallas import tpu as pltpu
from jax.sharding import PartitionSpec as P

DEGREE = 8
CHUNKS = 2

lowest = -1.0
cutoff = 1.5
ceiling = 4.5
eps_norm = 1e-06

F32 = jnp.float32
BF16 = jnp.bfloat16
VMEM = pl.BlockSpec(memory_space=pltpu.VMEM)
SMEM = pl.BlockSpec(memory_space=pltpu.SMEM)
LIMIT = 10 * 1024 * 1024


def up_to(value, unit):
    return -(-value // unit) * unit


def split(value):
    high = value.astype(BF16)
    return high, (value - high.astype(F32)).astype(BF16)


def mm(left, right):
    return jnp.dot(left, right, preferred_element_type=F32)


def mm_nt(left, right):
    return lax.dot_general(left, right, (((1,), (1,)), ((), ())), preferred_element_type=F32)


def shifted(shard, axis, by):
    count = lax.axis_size(axis)
    pairs = [(i, i + by) for i in range(count) if 0 <= i + by < count]
    return lax.ppermute(shard, axis, pairs)


def coefficients():
    half_width = (ceiling - cutoff) / 2.0
    centre = (ceiling + cutoff) / 2.0
    sigma_one = half_width / (lowest - centre)
    pairs = [(sigma_one / half_width, 0.0)]
    sigma_now = sigma_one
    for _ in range(DEGREE - 1):
        sigma_next = 1.0 / (2.0 / sigma_one - sigma_now)
        pairs.append((2.0 * sigma_next / half_width, sigma_now * sigma_next))
        sigma_now = sigma_next
    return centre, pairs


class Layout:
    def __init__(self, owned, face):
        self.owned = owned
        self.face = face
        self.rest = up_to(owned - face, 8)
        self.fpad = up_to(face, 8)
        self.rows = up_to(self.rest + self.fpad, 16)
        self.ext = up_to(self.rows + self.fpad, 16)
        self.whole = face // 8 * 8
        self.part = face - self.whole

    def packed(self, width):
        lanes = min(width, 128)
        groups = width // lanes
        return groups, lanes, groups * self.whole + up_to(groups * self.part, 8)

    def pack(self, ref, value):
        groups, lanes, _ = self.packed(value.shape[1])
        for group in range(groups):
            columns = value[:, group * lanes : (group + 1) * lanes]
            ref[group * self.whole : (group + 1) * self.whole] = columns[: self.whole]
            at = groups * self.whole + group * self.part
            if self.part:
                ref[at : at + self.part] = columns[self.whole : self.face]
        used = groups * self.face
        if ref.shape[0] > used:
            ref[used:] = jnp.zeros((ref.shape[0] - used, lanes), F32)

    def unpack(self, ref, width):
        groups, lanes, _ = self.packed(width)
        parts = []
        for group in range(groups):
            pieces = [ref[group * self.whole : (group + 1) * self.whole]]
            at = groups * self.whole + group * self.part
            if self.part:
                pieces.append(ref[at : at + self.part])
            pieces.append(jnp.zeros((self.fpad - self.face, lanes), F32))
            parts.append(jnp.concatenate(pieces, axis=0))
        return jnp.concatenate(parts, axis=1) if groups > 1 else parts[0]

    def position(self, ids, faces):
        same = ids[:, None] == faces[None, :]
        slot = jnp.sum(jnp.where(same, jnp.arange(self.face, dtype=jnp.int32)[None, :] + 1, 0), axis=1)
        below = jnp.sum((faces[None, :] < ids[:, None]).astype(jnp.int32), axis=1)
        own = jnp.where(slot > 0, self.rest + slot - 1, ids - below)
        return jnp.where(ids < self.owned, own, self.rows + ids - self.owned)


def arrange_kernel(lay, a_ref, q_ref, bh_ref, bl_ref, gh_ref, gl_ref, corner_ref):
    cells, nodes, _ = a_ref.shape
    total = jnp.zeros((lay.ext, lay.ext), F32)
    for cell in range(cells):
        q = q_ref[cell]
        hot = (lax.broadcasted_iota(jnp.int32, (lay.ext, nodes), 0) == q).astype(F32).astype(BF16)
        for part in split(a_ref[cell]):
            total = total + mm_nt(mm(hot, part).astype(BF16), hot)
    bh_ref[...], bl_ref[...] = split(total[: lay.rows])
    lower = total[lay.rows : lay.rows + lay.fpad]
    gh_ref[...], gl_ref[...] = split(lower[:, : lay.rows])
    corner_ref[...] = lower[:, lay.rows : lay.rows + lay.fpad]


def arrange(lay, matrices, q):
    own = jax.ShapeDtypeStruct((lay.rows, lay.ext), BF16)
    ghost = jax.ShapeDtypeStruct((lay.fpad, lay.rows), BF16)
    return pl.pallas_call(
        lambda *refs: arrange_kernel(lay, *refs),
        out_shape=[own, own, ghost, ghost, jax.ShapeDtypeStruct((lay.fpad, lay.fpad), F32)],
        in_specs=[VMEM, VMEM],
        out_specs=[VMEM] * 5,
        compiler_params=pltpu.CompilerParams(vmem_limit_bytes=LIMIT),
        name="arrange",
    )(matrices, q)


def patch_kernel(lay, corner_ref, high_ref, low_ref, new_high_ref, new_low_ref):
    at = slice(lay.rest, lay.rest + lay.fpad)
    value = high_ref[at, at].astype(F32) + low_ref[at, at].astype(F32) + corner_ref[...]
    new_high_ref[...], new_low_ref[...] = high_ref[...], low_ref[...]
    new_high_ref[at, at], new_low_ref[at, at] = split(value)


def patch(lay, corner, high, low):
    own = jax.ShapeDtypeStruct((lay.rows, lay.ext), BF16)
    return pl.pallas_call(
        lambda *refs: patch_kernel(lay, *refs),
        out_shape=[own, own],
        in_specs=[VMEM] * 3,
        out_specs=[VMEM] * 2,
        compiler_params=pltpu.CompilerParams(vmem_limit_bytes=LIMIT),
        name="patch",
    )(corner, high, low)


def outgoing(lay, odd_ref, gh_ref, gl_ref, value, near_ref, far_ref):
    high, low = split(value)
    gh = gh_ref[...]
    lift = mm(gh, high) + mm(gh, low) + mm(gl_ref[...], high)
    face = value[lay.rest : lay.rest + lay.fpad]
    even = odd_ref[0] == 0
    lay.pack(near_ref, jnp.where(even, lift, face))
    lay.pack(far_ref, jnp.where(even, face, lift))


def rows_of(lay, place_ref):
    ids = lax.broadcasted_iota(jnp.int32, (lay.rows, lay.owned), 0)
    return (ids == place_ref[...]).astype(F32).astype(BF16)


def first_kernel(lay, at, odd_ref, place_ref, gh_ref, gl_ref, raw_ref, cur_ref, near_ref, far_ref):
    hot = rows_of(lay, place_ref)
    raw = raw_ref[:, at : at + cur_ref.shape[1]]
    high, low = split(raw)
    rest = (raw - high.astype(F32) - low.astype(F32)).astype(BF16)
    cur_ref[...] = mm(hot, high) + mm(hot, low) + mm(hot, rest)
    outgoing(lay, odd_ref, gh_ref, gl_ref, cur_ref[...], near_ref, far_ref)


def step_kernel(
    lay, centre, alpha, beta, last, odd_ref, bh_ref, bl_ref, gh_ref, gl_ref, cur_ref, prev_ref, near_ref, far_ref, *outs
):
    new_ref = outs[0]
    high_ref, low_ref = outs[-2:]
    rows, width = cur_ref.shape
    high_ref[:rows], low_ref[:rows] = split(cur_ref[...])
    even = odd_ref[0] == 0
    near, far = lay.unpack(near_ref, width), lay.unpack(far_ref, width)
    ghost, add = jnp.where(even, near, far), jnp.where(even, far, near)
    if lay.ext - rows > lay.fpad:
        ghost = jnp.concatenate([ghost, jnp.zeros((lay.ext - rows - lay.fpad, width), F32)], axis=0)
    high_ref[rows:], low_ref[rows:] = split(ghost)
    block = min(width, 256)

    @pl.loop(0, width // block)
    def _(index):
        columns = pl.ds(pl.multiple_of(index * block, block), block)
        high = high_ref[:, columns]
        value = mm(bh_ref[...], high) + mm(bh_ref[...], low_ref[:, columns]) + mm(bl_ref[...], high)
        new = (value - centre * cur_ref[:, columns]) * alpha
        if beta:
            new = new - beta * prev_ref[:, columns]
        new_ref[:, columns] = new

    new_ref[lay.rest : lay.rest + lay.fpad] += alpha * add
    if last:
        for at, end in ((lay.owned - lay.face, lay.rest), (lay.rest + lay.face, rows)):
            if end > at:
                new_ref[at:end] = jnp.zeros((end - at, width), F32)
    else:
        outgoing(lay, odd_ref, gh_ref, gl_ref, new_ref[...], outs[1], outs[2])


def cost(lay, width):
    return pl.CostEstimate(
        flops=6 * lay.ext * lay.ext * width, bytes_accessed=3 * 4 * lay.rows * width, transcendentals=0
    )


def message(lay, width):
    _, lanes, height = lay.packed(width)
    return jax.ShapeDtypeStruct((height, lanes), F32)


def first(lay, odd, place, gh, gl, raw, at, width):
    return pl.pallas_call(
        lambda *refs: first_kernel(lay, at, *refs),
        out_shape=[jax.ShapeDtypeStruct((lay.rows, width), F32)] + [message(lay, width)] * 2,
        in_specs=[SMEM] + [VMEM] * 4,
        out_specs=[VMEM] * 3,
        compiler_params=pltpu.CompilerParams(vmem_limit_bytes=2 * LIMIT),
        cost_estimate=cost(lay, width),
        name="first",
    )(odd, place, gh, gl, raw)


def advance(lay, centre, alpha, beta, last, odd, matrices, cur, prev, near, far):
    width = cur.shape[1]
    outs = [jax.ShapeDtypeStruct((lay.rows, width), F32)]
    if not last:
        outs += [message(lay, width)] * 2
    return pl.pallas_call(
        lambda *refs: step_kernel(lay, centre, alpha, beta, last, *refs),
        out_shape=outs,
        in_specs=[SMEM] + [VMEM] * 8,
        out_specs=[VMEM] * len(outs),
        scratch_shapes=[pltpu.VMEM((lay.ext, width), BF16)] * 2,
        compiler_params=pltpu.CompilerParams(vmem_limit_bytes=LIMIT),
        cost_estimate=cost(lay, width),
        name="step",
    )(odd, *matrices, cur, prev, near, far)


def neighbours(value, begin):
    count = lax.axis_size("nodes")
    pairs = []
    for low in range(begin, count - 1, 2):
        pairs += [(low, low + 1), (low + 1, low)]
    return lax.ppermute(value, "nodes", pairs)


def filter_chunks(lay, matrices, place, orbitals):
    centre, pairs = coefficients()
    odd = (lax.axis_index("nodes") % 2).reshape(1).astype(jnp.int32)
    states = []
    width = orbitals.shape[1] // CHUNKS
    for chunk in range(CHUNKS):
        cur, near, far = first(lay, odd, place, matrices[2], matrices[3], orbitals, chunk * width, width)
        states.append((cur, cur, near, far))
    for degree, (alpha, beta) in enumerate(pairs):
        last = degree == len(pairs) - 1
        fresh = []
        for cur, prev, near, far in states:
            near, far = neighbours(near, 0), neighbours(far, 1)
            outs = advance(lay, centre, alpha, beta, last, odd, matrices, cur, prev, near, far)
            fresh.append((outs[0], cur) + tuple(outs[1:]))
        states = fresh
    return [state[0] for state in states]


def inner(left, right):
    return jnp.einsum("no,nq->oq", left, right, precision=lax.Precision.HIGH)


def orthonormalize_ring(filtered, place, owned):
    width = filtered.shape[1]
    total_rows = owned * lax.axis_size("nodes")
    members = lax.axis_size("orb")
    position = lax.axis_index("orb")
    blocks = [filtered]
    for stride in range(1, members // 2 + 1):
        pairs = [(source, (source + stride) % members) for source in range(members)]
        blocks.append(lax.ppermute(filtered, "orb", pairs))
    tiles = lax.psum(jnp.stack([inner(filtered, block) for block in blocks]), "nodes")
    eye = jnp.eye(width, dtype=jnp.bool_)
    diag_own = jnp.sum(jnp.where(eye, tiles[0], 0.0), axis=0)
    diag_all = lax.all_gather(diag_own, "orb", axis=0, tiled=True)
    scale_all = lax.rsqrt(diag_all / total_rows + eps_norm)
    scale_own = lax.rsqrt(diag_own / total_rows + eps_norm)
    unit_own = filtered * scale_own[None, :]
    mixed = jnp.zeros(filtered.shape, F32)
    for stride in range(members // 2 + 1):
        source = (position - stride) % members
        scale_source = lax.dynamic_slice_in_dim(scale_all, source * width, width, 0)
        coupling = tiles[stride] * scale_own[:, None] * scale_source[None, :] / total_rows
        mixed = mixed + jnp.dot(
            blocks[stride] * scale_source[None, :], coupling.T, precision=lax.Precision.HIGH
        )
        if stride > 0 and 2 * stride != members:
            returned = jnp.dot(unit_own, coupling, precision=lax.Precision.HIGH)
            pairs = [(source, (source - stride) % members) for source in range(members)]
            mixed = mixed + lax.ppermute(returned, "orb", pairs)
    rotated = 1.5 * unit_own - 0.5 * mixed
    return rotated[place]


def mm_tn(left, right):
    return lax.dot_general(left, right, (((0,), (0,)), ((), ())), preferred_element_type=F32)


def triple(product, left, right):
    return product(left[0], right[0]) + product(left[0], right[1]) + product(left[1], right[0])


QUARTERS = 4
OWN_BLOCKS = 10
CROSS_BLOCKS = 8
ORDERS = 3


def columns_of(quarter, bs):
    if isinstance(quarter, int):
        return slice(quarter * bs, (quarter + 1) * bs)
    return pl.ds(pl.multiple_of(quarter * bs, bs), bs)


def own_pairs(visit):
    for first, number, ahead in ((0, 4, 0), (4, 4, 1), (8, 2, 2)):
        for row in range(number):
            visit(first + row, row, (row + ahead) % QUARTERS, ahead)


def own_gram_kernel(bs, a_ref, b_ref, out_ref, norm_ref, high_ref, low_ref):
    half = 2 * bs
    norm_ref[...] = jnp.zeros_like(norm_ref)
    for quarter in range(QUARTERS):
        value = (a_ref, b_ref)[quarter // 2][:, columns_of(quarter % 2, bs)]
        norm_ref[quarter : quarter + 1] = jnp.sum(value * value, axis=0, keepdims=True)
    high_ref[:, :half], low_ref[:, :half] = split(a_ref[...])
    high_ref[:, half:], low_ref[:, half:] = split(b_ref[...])

    def visit(slot, row, column, ahead):
        left = high_ref[:, columns_of(row, bs)], low_ref[:, columns_of(row, bs)]
        right = high_ref[:, columns_of(column, bs)], low_ref[:, columns_of(column, bs)]
        out_ref[columns_of(slot, bs)] = triple(mm_tn, left, right)

    own_pairs(visit)


def cross_gram_kernel(bs, o_ref, a_ref, b_ref, oa_ref, ob_ref, out_ref, high_ref, low_ref, oh_ref, ol_ref):
    half = 2 * bs
    for index, (ref, high, low) in enumerate(
        ((a_ref, high_ref, low_ref), (b_ref, high_ref, low_ref), (oa_ref, oh_ref, ol_ref), (ob_ref, oh_ref, ol_ref))
    ):
        value = ref[...]
        at = slice(index % 2 * half, (index % 2 + 1) * half)
        high[:, at], low[:, at] = split(value)
    core = o_ref[0]

    for quarter in range(QUARTERS):
        facing = lax.bitwise_xor(quarter // 2, core)
        left = high_ref[:, columns_of(quarter, bs)], low_ref[:, columns_of(quarter, bs)]
        right = oh_ref[:, columns_of(facing, half)], ol_ref[:, columns_of(facing, half)]
        rows = triple(mm_tn, left, right)
        for k in range(2):
            out_ref[columns_of(2 * quarter + k, bs)] = rows[:, k * bs : (k + 1) * bs]


def own_gram(a, b, bs):
    return pl.pallas_call(
        lambda *refs: own_gram_kernel(bs, *refs),
        out_shape=[jax.ShapeDtypeStruct((OWN_BLOCKS * bs, bs), F32), jax.ShapeDtypeStruct((8, bs), F32)],
        in_specs=[VMEM] * 2,
        out_specs=[VMEM] * 2,
        scratch_shapes=[pltpu.VMEM((a.shape[0], 4 * bs), BF16)] * 2,
        compiler_params=pltpu.CompilerParams(vmem_limit_bytes=LIMIT),
        cost_estimate=pl.CostEstimate(flops=6 * 10 * a.shape[0] * bs * bs, bytes_accessed=4 * a.size, transcendentals=0),
        name="own_gram",
    )(a, b)


def cross_gram(core, a, b, oa, ob, bs):
    return pl.pallas_call(
        lambda *refs: cross_gram_kernel(bs, *refs),
        out_shape=jax.ShapeDtypeStruct((CROSS_BLOCKS * bs, bs), F32),
        in_specs=[SMEM] + [VMEM] * 4,
        out_specs=VMEM,
        scratch_shapes=[pltpu.VMEM((a.shape[0], 4 * bs), BF16)] * 4,
        compiler_params=pltpu.CompilerParams(vmem_limit_bytes=LIMIT),
        cost_estimate=pl.CostEstimate(flops=6 * 8 * a.shape[0] * bs * bs, bytes_accessed=8 * a.size, transcendentals=0),
        name="cross_gram",
    )(core, a, b, oa, ob)


def weigh_kernel(lay, bs, total_rows, norm_ref, other_ref, place_ref, *refs):
    sources, (wh_ref, wl_ref, back_ref, scale_ref) = refs[:4], refs[4:]
    hot = rows_of(lay, place_ref)
    for quarter in range(2 * QUARTERS):
        norm = (norm_ref, other_ref)[quarter // QUARTERS][quarter % QUARTERS : quarter % QUARTERS + 1]
        scale = lax.rsqrt(norm / total_rows + eps_norm)
        value = sources[quarter // 2][:, quarter % 2 * bs : (quarter % 2 + 1) * bs]
        at = slice(quarter * bs, (quarter + 1) * bs)
        high, low = split(value * (scale * scale * (0.5 / total_rows)))
        wh_ref[:, at], wl_ref[:, at] = mm_tn(hot, high).astype(BF16), mm_tn(hot, low).astype(BF16)
        if quarter < QUARTERS:
            back_ref[:, at] = 1.5 / (scale * scale * (0.5 / total_rows))
            scale_ref[:, at] = scale


def weigh(lay, norms, others, place, sources, bs, total_rows):
    width = 2 * sources[0].shape[1]
    return pl.pallas_call(
        lambda *refs: weigh_kernel(lay, bs, total_rows, *refs),
        out_shape=[
            jax.ShapeDtypeStruct((lay.owned, 2 * width), BF16),
            jax.ShapeDtypeStruct((lay.owned, 2 * width), BF16),
            jax.ShapeDtypeStruct((1, width), F32),
            jax.ShapeDtypeStruct((1, width), F32),
        ],
        in_specs=[VMEM] * 7,
        out_specs=[VMEM] * 4,
        compiler_params=pltpu.CompilerParams(vmem_limit_bytes=LIMIT),
        cost_estimate=pl.CostEstimate(
            flops=8 * lay.owned * lay.rows * width, bytes_accessed=24 * lay.owned * width, transcendentals=0
        ),
        name="weigh",
    )(norms, others, place, *sources)


def rotate_own_kernel(bs, wh_ref, wl_ref, back_ref, t_ref, out_ref):
    for quarter in range(QUARTERS):
        at = columns_of(quarter, bs)
        out_ref[:, at] = (wh_ref[:, at].astype(F32) + wl_ref[:, at].astype(F32)) * back_ref[:, at]

    def weight(quarter):
        return wh_ref[:, columns_of(quarter, bs)], wl_ref[:, columns_of(quarter, bs)]

    def visit(slot, row, column, ahead):
        block = split(t_ref[columns_of(slot, bs)])
        out_ref[:, columns_of(column, bs)] -= triple(mm, weight(row), block)
        if ahead:
            out_ref[:, columns_of(row, bs)] -= triple(mm_nt, weight(column), block)

    own_pairs(visit)


def rotate_cross_kernel(bs, o_ref, wh_ref, wl_ref, base_ref, scale_ref, x_ref, p_ref, out_ref):
    core = o_ref[0]

    def weight(quarter):
        return wh_ref[:, columns_of(quarter, bs)], wl_ref[:, columns_of(quarter, bs)]

    @pl.loop(0, QUARTERS)
    def _(j):
        half = lax.shift_right_logical(j, 1)
        inside = lax.bitwise_and(j, 1)
        facing = lax.bitwise_xor(half, core)
        across = 1 - facing
        total = base_ref[:, columns_of(j, bs)]
        for k in range(2):
            mine = split(x_ref[columns_of(half * 4 + inside * 2 + k, bs)])
            total = total - triple(mm_nt, weight(QUARTERS + 2 * facing + k), mine)
            theirs = split(p_ref[columns_of(across * 4 + k * 2 + inside, bs)])
            total = total - triple(mm, weight(QUARTERS + 2 * across + k), theirs)
        out_ref[:, columns_of(j, bs)] = total * scale_ref[:, columns_of(j, bs)]


def rotate_own(wh, wl, back, blocks, bs):
    rows, width = wh.shape[0], back.shape[1]
    return pl.pallas_call(
        lambda *refs: rotate_own_kernel(bs, *refs),
        out_shape=jax.ShapeDtypeStruct((rows, width), F32),
        in_specs=[VMEM] * 4,
        out_specs=VMEM,
        compiler_params=pltpu.CompilerParams(vmem_limit_bytes=LIMIT),
        cost_estimate=pl.CostEstimate(flops=6 * rows * width * width, bytes_accessed=8 * rows * width, transcendentals=0),
        name="rotate_own",
    )(wh, wl, back, blocks)


def rotate_cross(core, wh, wl, base, scale, blocks, partner, bs):
    rows, width = base.shape
    return pl.pallas_call(
        lambda *refs: rotate_cross_kernel(bs, *refs),
        out_shape=jax.ShapeDtypeStruct((rows, width), F32),
        in_specs=[SMEM] + [VMEM] * 6,
        out_specs=VMEM,
        compiler_params=pltpu.CompilerParams(vmem_limit_bytes=LIMIT),
        cost_estimate=pl.CostEstimate(flops=6 * rows * width * width, bytes_accessed=8 * rows * width, transcendentals=0),
        name="rotate_cross",
    )(core, wh, wl, base, scale, blocks, partner)


def exchange(value, axis, bit):
    count = lax.axis_size(axis)
    return lax.ppermute(value, axis, [(i, i ^ (1 << bit)) for i in range(count)])


def side(node, bit):
    return (node >> bit) & 1


def fold_kernel(summed, carries, whole, sizes, *refs):
    refs = list(refs)
    sides_ref = None if whole else refs.pop(0)
    starts = [0] * ORDERS
    if summed:
        keeps, gots, refs = refs[:ORDERS], refs[ORDERS : 2 * ORDERS], refs[2 * ORDERS :]
    else:
        keeps, gots, refs = [refs[0]] * ORDERS, [None] * ORDERS, refs[1:]
        starts = [sum(sizes[:index]) for index in range(ORDERS)]
    norms = None
    if carries:
        norm_ref, refs = refs[0], refs[1:]
        norms = norm_ref[...]
        if summed:
            norms = norms + gots[-1][sizes[-1] :]

    def rows(index, at):
        value = keeps[index][at]
        return value + gots[index][at] if summed else value

    if whole:
        at = 0
        for index in range(ORDERS):
            size = sizes[index]
            refs[0][at : at + size] = rows(index, slice(0, size))
            at += size
        if carries:
            refs[0][at:] = norms
        return
    aways, kept = refs[:ORDERS], refs[ORDERS : 2 * ORDERS]
    for index in range(ORDERS):
        half = kept[index].shape[0]
        mine = pl.multiple_of(starts[index] + sides_ref[index] * half, 8)
        theirs = pl.multiple_of(starts[index] + (1 - sides_ref[index]) * half, 8)
        aways[index][:half] = rows(index, pl.ds(theirs, half))
        kept[index][...] = rows(index, pl.ds(mine, half))
    if carries:
        aways[-1][kept[-1].shape[0] :] = norms
        refs[2 * ORDERS][...] = norms


def fold(sides, keeps, gots, norms, whole, sizes):
    columns = keeps[0].shape[1]
    extra = 0 if norms is None else norms.shape[0]
    shape = lambda size: jax.ShapeDtypeStruct((size, columns), F32)
    if whole:
        outs = [shape(sum(sizes) + extra)]
    else:
        halves = [size // 2 for size in sizes]
        outs = [shape(half) for half in halves[:-1]] + [shape(halves[-1] + extra)]
        outs += [shape(half) for half in halves] + ([shape(extra)] if extra else [])
    operands = keeps + (gots or []) + ([norms] if extra else [])
    return pl.pallas_call(
        lambda *refs: fold_kernel(bool(gots), bool(extra), whole, sizes, *refs),
        out_shape=outs,
        in_specs=([] if whole else [SMEM]) + [VMEM] * len(operands),
        out_specs=[VMEM] * len(outs),
        compiler_params=pltpu.CompilerParams(vmem_limit_bytes=LIMIT),
        cost_estimate=pl.CostEstimate(flops=keeps[0].size, bytes_accessed=24 * keeps[0].size, transcendentals=0),
        name="fold",
    )(*([] if whole else [sides]), *operands)


class Stream:
    def __init__(self, value, extra=None):
        count = lax.axis_size("nodes")
        self.node = lax.axis_index("nodes").astype(jnp.int32)
        bits = list(range(count.bit_length() - 1))
        self.last = bits.pop()
        self.phases = len(bits)
        self.orders = [bits[turn % len(bits) :] + bits[: turn % len(bits)] for turn in range(ORDERS)]
        unit = 8 << self.phases
        units = value.shape[0] // unit
        sizes = [units // ORDERS + (index < units % ORDERS) for index in range(ORDERS)]
        self.sizes = [size * unit for size in sizes]
        self.values = [value]
        self.extra = extra
        self.got = None

    def scatter_start(self, phase):
        sides = jnp.stack([side(self.node, order[phase]) for order in self.orders])
        outs = fold(sides, self.values, self.got, self.extra, False, self.sizes)
        self.sizes = [size // 2 for size in self.sizes]
        self.values = list(outs[ORDERS : 2 * ORDERS])
        if self.extra is not None:
            self.extra = outs[2 * ORDERS]
        self.got = [exchange(value, "nodes", order[phase]) for value, order in zip(outs, self.orders)]

    def middle_start(self):
        self.whole = fold(None, self.values, self.got, self.extra, True, self.sizes)[0]
        self.got = exchange(self.whole, "nodes", self.last)

    def middle_done(self):
        total, at, parts = self.whole + self.got, 0, []
        for value in self.values:
            parts.append(total[at : at + value.shape[0]])
            at += value.shape[0]
        self.values = parts
        if self.extra is not None:
            self.extra = total[at:]

    def gather_start(self, phase):
        self.got = [exchange(value, "nodes", order[phase]) for value, order in zip(self.values, self.orders)]
        self.phase = phase

    def gather_done(self):
        self.got = lax.optimization_barrier(self.got)
        values = []
        for value, got, order in zip(self.values, self.got, self.orders):
            lower = side(self.node, order[self.phase]) == 0
            values += [jnp.where(lower, value, got), jnp.where(lower, got, value)]
        if self.phase == 0:
            self.values = [jnp.concatenate(values, axis=0)]
        else:
            self.values = [jnp.concatenate(values[2 * i : 2 * i + 2], axis=0) for i in range(ORDERS)]


def orthonormalize_pair(lay, a, b, place, bs):
    core = lax.axis_index("orb")
    index = core.reshape(1).astype(jnp.int32)
    oa, ob = exchange(a, "orb", 0), exchange(b, "orb", 0)
    together = lax.optimization_barrier
    own = Stream(*own_gram(a, b, bs))
    own.scatter_start(0)
    blocks = cross_gram(index, a, b, oa, ob, bs)
    own.got, blocks = together((own.got, blocks))
    cross = Stream(blocks)
    cross.scatter_start(0)
    for phase in range(1, own.phases):
        own.scatter_start(phase)
        cross.scatter_start(phase)
    own.middle_start()
    cross.middle_start()
    own.middle_done()
    others = exchange(own.extra, "orb", 0)
    weights = weigh(lay, own.extra, others, place, (a, b, oa, ob), bs, lay.owned * lax.axis_size("nodes"))
    for phase in reversed(range(own.phases)):
        own.gather_start(phase)
        if phase == own.phases - 1:
            cross.got, weights = together((cross.got, weights))
            cross.middle_done()
        else:
            cross.gather_done()
        cross.gather_start(phase)
        own.gather_done()
    wh, wl, back, scale = weights
    base = rotate_own(wh, wl, back, own.values[0], bs)
    cross.got, base = together((cross.got, base))
    cross.gather_done()
    partner = exchange(cross.values[0], "orb", 0)
    return rotate_cross(index, wh, wl, base, scale, cross.values[0], partner, bs)


def body(orbitals, cell_matrix, connectivity, face_nodes):
    owned, width = orbitals.shape
    lay = Layout(owned, face_nodes.shape[0])
    cells, nodes = connectivity.shape
    place = lay.position(jnp.arange(owned, dtype=jnp.int32), face_nodes)
    q = lay.position(connectivity.reshape(-1), face_nodes).reshape(cells, 1, nodes)
    spot = place.reshape(1, owned)
    bh, bl, gh, gl, corner = arrange(lay, cell_matrix, q)
    matrices = (*patch(lay, shifted(corner, "nodes", 1), bh, bl), gh, gl)

    parts = filter_chunks(lay, matrices, spot, orbitals)
    count = lax.axis_size("nodes")
    bs = width // QUARTERS
    if lax.axis_size("orb") == 2 and CHUNKS == 2 and count & (count - 1) == 0 and count > 2 and bs % 128 == 0 and 2 * bs % (4 * count) == 0:
        return orthonormalize_pair(lay, parts[0], parts[1], spot, bs)
    return orthonormalize_ring(jnp.concatenate(parts, axis=1), place, owned)


def solution(mesh):
    return jax.shard_map(
        body,
        mesh=mesh,
        in_specs=(P("nodes", "orb"), P("nodes", None, None), P("nodes", None), P("nodes")),
        out_specs=P("nodes", "orb"),
        check_vma=False,
    )
```
